256 devices in a mesh: row: 32 (over x_hi, z, core), col: 8 (over x_lo, y).
Axes of the slice: x: 4 (x_hi: 2, x_lo: 2; x = x_hi * 2 + x_lo), y: 4, z: 8, core: 2. Of those that a mesh axis runs over, the one named last changes fastest.
Arguments:
- pair: bfloat16 [64, 2048, 2048], P(None, 'row', 'col'), may hold values from -6 to 6
- conv_weight: bfloat16 [9, 64, 64], replicated, may hold values from -0.25 to 0.25
- conv_bias: float32 [64], replicated, may hold values from -3 to 3
- single: bfloat16 [2048, 384], P('col'), may hold values from -6 to 6
- quat_vec: float32 [3, 2048], P(None, 'col'), may hold values from -6 to 6
- trans: float32 [3, 2048], P(None, 'col'), may hold values from -200 to 200
- chain_id: int32 [2048], P('col'), may hold values from 0 to 7, never falling along the last dimension, each value on 1 to 512 neighbouring positions
- residue_mask: int32 [2048], P('col'), may hold values 0 or 1
- w_query: bfloat16 [384, 192], replicated, may hold values from -0.3125 to 0.3125
- w_key: bfloat16 [384, 192], replicated, may hold values from -0.3125 to 0.3125
- w_value: bfloat16 [384, 192], replicated, may hold values from -0.3125 to 0.3125
- w_qpts: bfloat16 [384, 144], replicated, may hold values from -0.3125 to 0.3125
- w_kvpts: bfloat16 [384, 432], replicated, may hold values from -0.3125 to 0.3125
- w_bias: bfloat16 [12, 64], replicated, may hold values from -0.75 to 0.75
- head_weight: float32 [12], replicated, may hold values from -1.5 to 1
- chain_weight: float32 [12], replicated, may hold values from -2 to 2
- w_out: bfloat16 [1248, 384], replicated, may hold values from -0.15625 to 0.15625
- ln_gain: float32 [384], replicated, may hold values from 0.5 to 1.5
Outputs:
- pair_out: bfloat16 [64, 2048, 2048], P(None, 'row', 'col')
- single_out: bfloat16 [2048, 384], P('row')
The draws below stay inside these ranges and needn't reach their ends.
All inputs are finite; a program needn't handle non-finite values. No bound on the sum of `residue_mask` on one device may be relied on, other than what follows from the above.
Results may differ from the reference program's by a relative error of at most 0.0034.
Values may be sent and summed in bfloat16 or wider, within the bound.
No kernel may reach another device: no remote copies, remote signals or barrier semaphores. Data moves between devices by JAX's collectives and lax.ppermute only.
A program may use at most 128 MiB of HBM per device.

```python
import math
import jax
import jax.numpy as jnp
import numpy as np
from jax import lax

C = 64
S = 384
H = 12
HD = 16
QP = 4
VP = 8
DILATION_STEP = 8
CHAINS = 8
N = 2048
TILE_ROWS = 64
N_ROW = 32


def draw_trans(key, part):
    key_spread = jax.random.fold_in(key, 0)
    return jnp.clip(2.0 * jax.random.normal(key_spread, (3, N), jnp.float32), -12.0, 12.0)


def set_ends(array, own_key, smallest, largest):
    extent = array.shape
    index_at = [jax.random.randint(jax.random.fold_in(own_key, axis), (), 0, extent[axis]) for axis in range(len(extent))]
    array = array.at[tuple(index_at)].set(smallest)
    longest = extent.index(max(extent))
    index_at[longest] = (index_at[longest] + 1) % extent[longest]
    return array.at[tuple(index_at)].set(largest)


def block_levels(stream_key, shape, shards, smallest, high):
    loudness, own = 1.0, jax.random.fold_in(stream_key, 6)
    for axis_at, shards_of in shards:
        steps = jnp.exp(jax.random.uniform(jax.random.fold_in(own, axis_at), (shards_of,), jnp.float32, smallest / len(shards), high / len(shards)))
        loudness = loudness * jnp.repeat(steps, shape[axis_at] // shards_of).reshape([-1 if axis == axis_at else 1 for axis in range(len(shape))])
    return loudness


def profile(count, total, reach, lean):
    weights = [(1 << 20) // math.isqrt(grade ** lean) + 1 for grade in range(2, count + 1)]
    spare, given = total - reach - (count - 1), [1] * (count - 1)
    while spare > 0:
        movable = [i for i in range(count - 1) if given[i] < reach]
        whole, budget = sum([weights[i] for i in movable]), spare
        for i in movable:
            extra = min(reach - given[i], max(1, budget * weights[i] // whole), spare)
            given[i] = given[i] + extra
            spare = spare - extra
    return np.array([reach] + given)


def ragged(rng, amount, total, reach, skew):
    if amount == 2:
        one = jax.random.randint(rng, (), max(1, total - reach), min(reach, total - 1) + 1)
        return jnp.stack([one, total - one])
    lengths = jnp.asarray(profile(amount, total, reach, skew), jnp.int32)
    couples = (amount - 1) // 2
    giver, receiver = lengths[1:1 + 2 * couples:2], lengths[2:2 + 2 * couples:2]
    margin = jnp.minimum(giver - 1, reach - receiver)
    passed = jax.random.randint(jax.random.fold_in(rng, 1), (couples,), 0, 1 << 20) % (margin + 1)
    lengths = lengths.at[1:1 + 2 * couples:2].set(giver - passed).at[2:2 + 2 * couples:2].set(receiver + passed)
    return lengths[jax.random.permutation(jax.random.fold_in(rng, 2), amount)]


def scatter_about(own_key, dims, width, bound, cuts=(), kind=jnp.bfloat16):
    gain = block_levels(own_key, dims, cuts, -0.22, 0.18) if cuts else 1.0
    array = jax.random.normal(own_key, dims, jnp.float32) * width * gain
    return jnp.minimum(jnp.maximum(array, -bound), bound).astype(kind)


def setup_inputs(seed: int = 0) -> dict:
    key_list = jax.random.split(jax.random.key(seed), 19)
    pair = scatter_about(key_list[0], (C, N, N), 1.0, 6.0, ((1, 32), (2, 8)))
    conv_weight = scatter_about(key_list[1], (9, C, C), (9 * C) ** -0.5, 0.25)
    conv_bias = scatter_about(key_list[2], (C,), 0.5, 3.0, (), jnp.float32)
    single = scatter_about(key_list[3], (N, S), 1.0, 6.0, ((0, 8),))
    quat_vec = scatter_about(key_list[4], (3, N), 1.0, 6.0, ((1, 8),), jnp.float32)
    trans = draw_trans(jax.random.fold_in(key_list[18], 71), 0)
    chain_id = jnp.searchsorted(jnp.cumsum(ragged(key_list[6], CHAINS, N, N // 4, 1)), jnp.arange(N), side="right").astype(jnp.int32)
    residue_mask = set_ends((jax.random.randint(key_list[7], (N,), 0, 8) < 7).astype(jnp.int32), jax.random.fold_in(key_list[7], 1), 0, 1)
    w_query = scatter_about(key_list[8], (S, H * HD), S ** -0.5, 0.3125)
    w_key = scatter_about(key_list[9], (S, H * HD), S ** -0.5, 0.3125)
    w_value = scatter_about(key_list[10], (S, H * HD), S ** -0.5, 0.3125)
    w_qpts = scatter_about(key_list[11], (S, 3 * H * QP), S ** -0.5, 0.3125)
    w_kvpts = scatter_about(key_list[12], (S, 3 * H * (QP + VP)), S ** -0.5, 0.3125)
    w_bias = scatter_about(key_list[13], (H, C), C ** -0.5, 0.75)
    head_weight = jnp.clip(jax.random.uniform(key_list[14], (H,), jnp.float32, -1.5, 1.0), -1.5, 1.0)
    chain_weight = jnp.clip(jax.random.uniform(key_list[15], (H,), jnp.float32, -2.0, 2.0), -2.0, 2.0)
    w_out = scatter_about(key_list[16], (H * (HD + C + 3 * VP), S), (H * (HD + C + 3 * VP)) ** -0.5, 0.15625)
    ln_gain = jnp.clip(1.0 + 0.1 * jax.random.normal(key_list[17], (S,), jnp.float32), 0.5, 1.5)
    return {"pair": pair, "conv_weight": conv_weight, "conv_bias": conv_bias, "single": single, "quat_vec": quat_vec, "trans": trans, "chain_id": chain_id, "residue_mask": residue_mask, "w_query": w_query, "w_key": w_key, "w_value": w_value, "w_qpts": w_qpts, "w_kvpts": w_kvpts, "w_bias": w_bias, "head_weight": head_weight, "chain_weight": chain_weight, "w_out": w_out, "ln_gain": ln_gain}


logit_scale = math.sqrt(1.0 / 3.0)
mask_penalty = 10000.0
norm_eps = 1e-05
highest = lax.Precision.HIGHEST

def rotations(quat_vec):
    comp_b = quat_vec[0]
    comp_c = quat_vec[1]
    comp_d = quat_vec[2]
    inverse_norm = 1.0 / (1.0 + comp_b * comp_b + comp_c * comp_c + comp_d * comp_d)
    first_row = jnp.stack([1.0 + comp_b * comp_b - comp_c * comp_c - comp_d * comp_d, 2.0 * (comp_b * comp_c - comp_d), 2.0 * (comp_b * comp_d + comp_c)])
    second_row = jnp.stack([2.0 * (comp_b * comp_c + comp_d), 1.0 - comp_b * comp_b + comp_c * comp_c - comp_d * comp_d, 2.0 * (comp_c * comp_d - comp_b)])
    third_row = jnp.stack([2.0 * (comp_b * comp_d - comp_c), 2.0 * (comp_c * comp_d + comp_b), 1.0 - comp_b * comp_b - comp_c * comp_c + comp_d * comp_d])
    return jnp.stack([first_row, second_row, third_row]) * inverse_norm

def project_points(single_rows, weight, head_count):
    flattened = jnp.dot(single_rows, weight, preferred_element_type=jnp.float32)
    count = single_rows.shape[0]
    return flattened.reshape(count, 3, head_count, -1).transpose(1, 2, 3, 0)

def globalize(local_points, rotation, shift):
    return jnp.einsum('xdn,dhpn->xhpn', rotation, local_points, precision=highest) + shift[:, None, None, :]

def reference(pair, conv_weight, conv_bias, single, quat_vec, trans, chain_id, residue_mask, w_query, w_key, w_value, w_qpts, w_kvpts, w_bias, head_weight, chain_weight, w_out, ln_gain):
    padded_pair = jnp.pad(pair, ((0, 0), (DILATION_STEP, DILATION_STEP), (DILATION_STEP, DILATION_STEP)))
    conv_w32 = conv_weight.astype(jnp.float32)

    def conv_rows(start_index):
        tile_window = lax.dynamic_slice_in_dim(padded_pair, start_index, TILE_ROWS + 2 * DILATION_STEP, 1)
        accumulated = jnp.zeros((C, TILE_ROWS, N), jnp.float32)
        for kernel_tap_index in range(9):
            row_shift = kernel_tap_index // 3 * DILATION_STEP
            column_shift = kernel_tap_index % 3 * DILATION_STEP
            window = tile_window[:, row_shift:row_shift + TILE_ROWS, column_shift:column_shift + N].astype(jnp.float32)
            accumulated = accumulated + jnp.einsum('oc,cij->oij', conv_w32[kernel_tap_index], window, precision=highest)
        initial = lax.dynamic_slice_in_dim(pair, start_index, TILE_ROWS, 1).astype(jnp.float32)
        return (initial + jax.nn.elu(accumulated + conv_bias[:, None, None])).astype(jnp.bfloat16)
    starts = jnp.arange(N_ROW, dtype=jnp.int32) * TILE_ROWS
    blocks = lax.map(conv_rows, starts)
    pair_out = blocks.transpose(1, 0, 2, 3).reshape(C, N, N)
    rotation = rotations(quat_vec)
    key_value_global = globalize(project_points(single, w_kvpts, H), rotation, trans)
    key_global = key_value_global[:, :, :QP]
    value_global = key_value_global[:, :, QP:]
    query_global = globalize(project_points(single, w_qpts, H), rotation, trans)
    queries = jnp.dot(single, w_query, preferred_element_type=jnp.float32).reshape(N, H, HD).transpose(1, 2, 0)
    key_rows = jnp.dot(single, w_key, preferred_element_type=jnp.float32).reshape(N, H, HD).transpose(1, 2, 0)
    values = jnp.dot(single, w_value, preferred_element_type=jnp.float32).astype(jnp.bfloat16).reshape(N, H, HD).transpose(1, 2, 0).astype(jnp.float32)
    point_scale = jax.nn.softplus(head_weight) * math.sqrt(2.0 / (9.0 * QP))
    query_feat = jnp.concatenate([queries / math.sqrt(HD), point_scale[:, None, None] * query_global.transpose(1, 0, 2, 3).reshape(H, 3 * QP, N)], axis=1)
    key_feat = jnp.concatenate([key_rows, key_global.transpose(1, 0, 2, 3).reshape(H, 3 * QP, N)], axis=1)
    query_sq = lax.optimization_barrier(jnp.sum(query_global * query_global, axis=(0, 2)))
    key_sq = lax.optimization_barrier(jnp.sum(key_global * key_global, axis=(0, 2)))
    present = residue_mask.astype(jnp.float32)
    w_bias32 = w_bias.astype(jnp.float32)
    w_out32 = w_out.astype(jnp.float32)

    def attend_rows(start_index):
        query_block = lax.dynamic_slice_in_dim(query_feat, start_index, TILE_ROWS, 2)
        query_sq_block = lax.dynamic_slice_in_dim(query_sq, start_index, TILE_ROWS, 1)
        pair_block = lax.dynamic_slice_in_dim(pair_out, start_index, TILE_ROWS, 1).astype(jnp.float32)
        chain_block = lax.dynamic_slice_in_dim(chain_id, start_index, TILE_ROWS, 0)
        rot_block = lax.dynamic_slice_in_dim(rotation, start_index, TILE_ROWS, 2)
        shift_block = lax.dynamic_slice_in_dim(trans, start_index, TILE_ROWS, 1)
        single_block = lax.dynamic_slice_in_dim(single, start_index, TILE_ROWS, 0).astype(jnp.float32)
        inner_products = jnp.einsum('hfi,hfj->hij', query_block, key_feat, precision=highest)
        pair_bias = jnp.einsum('hc,cij->hij', w_bias32, pair_block, precision=highest)
        same_chain = (chain_block[:, None] == chain_id[None, :]).astype(jnp.float32)
        logits = logit_scale * (inner_products + pair_bias - 0.5 * point_scale[:, None, None] * (query_sq_block[:, :, None] + key_sq[:, None, :]))
        logits = logits + chain_weight[:, None, None] * same_chain[None] - mask_penalty * (1.0 - present)[None, None, :]
        row_peak = lax.optimization_barrier(jnp.max(logits, axis=2))
        weights = jnp.exp(logits - row_peak[:, :, None]).astype(jnp.bfloat16).astype(jnp.float32)
        totals = lax.optimization_barrier(jnp.sum(weights, axis=2))
        scalar_sum = jnp.einsum('hij,hdj->hdi', weights, values, precision=highest)
        pair_sum = jnp.einsum('hij,cij->hci', weights, pair_block, precision=highest)
        point_sum = jnp.einsum('hij,xhpj->hxpi', weights, value_global, precision=highest)
        centred = point_sum / totals[:, None, None, :] - shift_block[None, :, None, :]
        local_points = jnp.einsum('xdi,hxpi->hdpi', rot_block, centred, precision=highest)
        features = jnp.concatenate([scalar_sum / totals[:, None, :], pair_sum / totals[:, None, :], local_points.reshape(H, 3 * VP, TILE_ROWS)], axis=1)
        flattened = features.transpose(2, 0, 1).reshape(TILE_ROWS, -1)
        update = jnp.dot(flattened, w_out32, precision=highest)
        hidden = single_block + update
        row_mean = lax.optimization_barrier(jnp.mean(hidden, axis=1, keepdims=True))
        row_var = lax.optimization_barrier(jnp.mean((hidden - row_mean) ** 2, axis=1, keepdims=True))
        return ((hidden - row_mean) * lax.rsqrt(row_var + norm_eps) * ln_gain[None, :]).astype(jnp.bfloat16)
    single_blocks = lax.map(attend_rows, starts)
    single_out = single_blocks.reshape(N, S)
    return (pair_out, single_out)
```

```python
import math

import jax
import jax.numpy as jnp
import numpy as np
from jax import lax
from jax.sharding import PartitionSpec as P

DILATION_STEP = 8


logit_scale = math.sqrt(1.0 / 3.0)
mask_penalty = 10000.0
norm_eps = 1e-05
highest = lax.Precision.HIGHEST


def with_halo(cells, sides, width):
    for axis, dim in sides:
        count = lax.axis_size(axis)
        ends = count - 1
        head = lax.slice_in_dim(cells, 0, width, axis=dim)
        tail = lax.slice_in_dim(cells, cells.shape[dim] - width, cells.shape[dim], axis=dim)
        cells = jnp.concatenate(
            [
                lax.ppermute(tail, axis, [(i, (i + 1) % count) for i in range(ends)]),
                cells,
                lax.ppermute(head, axis, [((i + 1) % count, i) for i in range(ends)]),
            ],
            axis=dim,
        )
    return cells


def ring(a, b, size):
    return min((a - b) % size, (b - a) % size)


def place(row, col, n_row, n_col):
    z_count = max(n_row // 4, 1)
    y_count = max(n_col // 2, 1)
    return (row // (2 * z_count) * 2 + col // y_count, col % y_count, row // 2 % z_count)


def query_routes(n_row, n_col):
    group = n_row // n_col
    z_count = max(n_row // 4, 1)
    y_count = max(n_col // 2, 1)
    pairs, offsets = [], np.zeros((n_row, n_col), np.int32)
    for holder_col in range(n_col):
        targets = [(holder_col * group + a, c) for a in range(group) for c in range(n_col)]
        sources = list(range(n_row))
        cost = np.zeros((n_row, n_row))
        for a, (row, col) in enumerate(targets):
            there = place(row, col, n_row, n_col)
            for b in sources:
                here = place(b, holder_col, n_row, n_col)
                hops = (
                    ring(there[0], here[0], 4)
                    + ring(there[1], here[1], y_count)
                    + ring(there[2], here[2], z_count)
                )
                cost[a, b] = float(hops) ** 4
        chosen = list(range(n_row))
        changed = True
        while changed:
            changed = False
            for a in range(n_row):
                for b in range(a):
                    now = cost[a, chosen[a]] + cost[b, chosen[b]]
                    then = cost[a, chosen[b]] + cost[b, chosen[a]]
                    if then < now - 1e-9:
                        chosen[a], chosen[b] = chosen[b], chosen[a]
                        changed = True
        for a, (row, col) in enumerate(targets):
            pairs.append((chosen[a] * n_col + holder_col, row * n_col + col))
            offsets[chosen[a], holder_col] = row % group
    return pairs, offsets


def pieces(value, count):
    parts = []
    for _ in range(count - 1):
        part = lax.reduce_precision(value, 8, 7)
        parts.append(part.astype(jnp.bfloat16))
        value = value - part
    parts.append(value.astype(jnp.bfloat16))
    return parts


def rotations(quat_vec):
    comp_b = quat_vec[0]
    comp_c = quat_vec[1]
    comp_d = quat_vec[2]
    inverse_norm = 1.0 / (1.0 + comp_b * comp_b + comp_c * comp_c + comp_d * comp_d)
    first_row = jnp.stack(
        [
            1.0 + comp_b * comp_b - comp_c * comp_c - comp_d * comp_d,
            2.0 * (comp_b * comp_c - comp_d),
            2.0 * (comp_b * comp_d + comp_c),
        ]
    )
    second_row = jnp.stack(
        [
            2.0 * (comp_b * comp_c + comp_d),
            1.0 - comp_b * comp_b + comp_c * comp_c - comp_d * comp_d,
            2.0 * (comp_c * comp_d - comp_b),
        ]
    )
    third_row = jnp.stack(
        [
            2.0 * (comp_b * comp_d - comp_c),
            2.0 * (comp_c * comp_d + comp_b),
            1.0 - comp_b * comp_b - comp_c * comp_c + comp_d * comp_d,
        ]
    )
    return jnp.stack([first_row, second_row, third_row]) * inverse_norm


def project_points(single_rows, weight, head_count):
    flattened = jnp.dot(single_rows, weight, preferred_element_type=jnp.float32)
    count = single_rows.shape[0]
    return flattened.reshape(count, 3, head_count, -1).transpose(1, 2, 3, 0)


def globalize(local_points, rotation, shift):
    return (
        jnp.einsum("xdn,dhpn->xhpn", rotation, local_points, precision=highest)
        + shift[:, None, None, :]
    )


def per_device(
    pair,
    conv_weight,
    conv_bias,
    single,
    quat_vec,
    trans,
    chain_id,
    residue_mask,
    w_query,
    w_key,
    w_value,
    w_qpts,
    w_kvpts,
    w_bias,
    head_weight,
    chain_weight,
    w_out,
    ln_gain,
):
    channels, row_count, col_count = pair.shape
    head_count = w_bias.shape[0]
    head_dim = w_query.shape[1] // head_count
    width = single.shape[1]
    query_points = w_qpts.shape[1] // (3 * head_count)
    value_points = w_kvpts.shape[1] // (3 * head_count) - query_points
    n_row, n_col = lax.axis_size("row"), lax.axis_size("col")
    part_count = row_count // n_col

    routes, offsets = query_routes(n_row, n_col)
    packed = jnp.concatenate([quat_vec, trans, chain_id.astype(jnp.float32)[None, :]], axis=0)
    offset = jnp.asarray(offsets)[lax.axis_index("row"), lax.axis_index("col")] * row_count
    mine_single = lax.dynamic_slice_in_dim(single, offset, row_count, 0)
    mine_frames = lax.dynamic_slice_in_dim(packed, offset, row_count, 1)
    frame_rows = jnp.concatenate(pieces(mine_frames, 3), axis=0)
    message = jnp.concatenate(
        [mine_single, jnp.pad(frame_rows, ((0, 3), (0, width - row_count)))], axis=0
    )
    message = lax.ppermute(message, ("row", "col"), routes)
    query_single = message[:row_count]
    frame_rows = message[row_count : row_count + 21, :row_count].astype(jnp.float32)
    query_frames = frame_rows[0:7] + frame_rows[7:14] + frame_rows[14:21]

    padded_pair = with_halo(pair, (("row", 1), ("col", 2)), DILATION_STEP)
    accumulated = jnp.zeros((channels, row_count, col_count), jnp.float32)
    for kernel_tap_index in range(9):
        row_shift = kernel_tap_index // 3 * DILATION_STEP
        column_shift = kernel_tap_index % 3 * DILATION_STEP
        window = padded_pair[
            :, row_shift : row_shift + row_count, column_shift : column_shift + col_count
        ]
        accumulated = accumulated + jnp.einsum(
            "oc,cij->oij", conv_weight[kernel_tap_index], window, preferred_element_type=jnp.float32
        )
    pair_out = (
        pair.astype(jnp.float32) + jax.nn.elu(accumulated + conv_bias[:, None, None])
    ).astype(jnp.bfloat16)
    key_rotation = rotations(quat_vec)
    key_value_global = globalize(project_points(single, w_kvpts, head_count), key_rotation, trans)
    key_global = key_value_global[:, :, :query_points]
    value_global = key_value_global[:, :, query_points:]
    key_rows = (
        jnp.dot(single, w_key, preferred_element_type=jnp.float32)
        .reshape(col_count, head_count, head_dim)
        .transpose(1, 2, 0)
    )
    values = (
        jnp.dot(single, w_value, preferred_element_type=jnp.float32)
        .astype(jnp.bfloat16)
        .reshape(col_count, head_count, head_dim)
        .transpose(1, 2, 0)
    )
    query_rotation = rotations(query_frames[0:3])
    query_shift = query_frames[3:6]
    query_chain = query_frames[6]
    query_global = globalize(
        project_points(query_single, w_qpts, head_count), query_rotation, query_shift
    )
    queries = (
        jnp.dot(query_single, w_query, preferred_element_type=jnp.float32)
        .reshape(row_count, head_count, head_dim)
        .transpose(1, 2, 0)
    )
    point_scale = jax.nn.softplus(head_weight) * math.sqrt(2.0 / (9.0 * query_points))
    query_feat = jnp.concatenate(
        [
            queries / math.sqrt(head_dim),
            point_scale[:, None, None]
            * query_global.transpose(1, 0, 2, 3).reshape(head_count, 3 * query_points, row_count),
        ],
        axis=1,
    )
    key_feat = jnp.concatenate(
        [
            key_rows,
            key_global.transpose(1, 0, 2, 3).reshape(head_count, 3 * query_points, col_count),
        ],
        axis=1,
    )
    query_sq = jnp.sum(query_global * query_global, axis=(0, 2))
    key_sq = jnp.sum(key_global * key_global, axis=(0, 2))
    inner_products = jnp.einsum("hfi,hfj->hij", query_feat, key_feat, precision=highest)
    pair_bias = jnp.einsum("hc,cij->hij", w_bias, pair_out, preferred_element_type=jnp.float32)
    same_chain = (query_chain[:, None] == chain_id.astype(jnp.float32)[None, :]).astype(jnp.float32)
    present = residue_mask.astype(jnp.float32)
    logits = logit_scale * (
        inner_products
        + pair_bias
        - 0.5 * point_scale[:, None, None] * (query_sq[:, :, None] + key_sq[:, None, :])
    )
    logits = (
        logits
        + chain_weight[:, None, None] * same_chain[None]
        - mask_penalty * (1.0 - present)[None, None, :]
    )
    own_peak = jnp.max(logits, axis=2)
    weights = jnp.exp(logits - own_peak[:, :, None]).astype(jnp.bfloat16)
    own_total = jnp.sum(weights.astype(jnp.float32), axis=2)
    scalar_sum = jnp.einsum("hij,hdj->ihd", weights, values, preferred_element_type=jnp.float32)
    pair_sum = jnp.einsum("hij,cij->ihc", weights, pair_out, preferred_element_type=jnp.float32)
    value_parts = pieces(value_global, 3)
    point_sum = sum(
        jnp.einsum("hij,xhpj->ihxp", weights, part, preferred_element_type=jnp.float32)
        for part in value_parts
    ).reshape(row_count, head_count, 3 * value_points)
    sums = jnp.concatenate(
        [
            pair_sum,
            scalar_sum,
            point_sum,
            own_peak.T[:, :, None],
            own_total.T[:, :, None],
        ],
        axis=2,
    )
    sums = jnp.pad(sums, ((0, 0), (0, 16 - head_count), (0, 128 - sums.shape[2])))
    sums = sums.reshape(n_col, part_count, 16, 128)
    sums = lax.all_to_all(sums, "col", 0, 0, tiled=False)[:, :, :head_count]
    used = channels + head_dim + 3 * value_points
    peaks = sums[..., used]
    scales = jnp.exp(peaks - jnp.max(peaks, axis=0, keepdims=True))
    totals = jnp.sum(sums[..., used + 1] * scales, axis=0)
    means = jnp.sum(sums[..., :used] * scales[..., None], axis=0) / totals[..., None]
    start = lax.axis_index("col") * part_count
    my_shift = lax.dynamic_slice_in_dim(query_shift, start, part_count, 1)
    my_rotation = lax.dynamic_slice_in_dim(query_rotation, start, part_count, 2)
    my_single = lax.dynamic_slice_in_dim(query_single, start, part_count, 0)
    global_points = means[..., channels + head_dim :].reshape(
        part_count, head_count, 3, value_points
    )
    centred = global_points - my_shift.T[:, None, :, None]
    local_points = jnp.einsum("xdi,ihxp->ihdp", my_rotation, centred, precision=highest)
    features = jnp.concatenate(
        [
            means[..., channels : channels + head_dim],
            means[..., :channels],
            local_points.reshape(part_count, head_count, -1),
        ],
        axis=2,
    )
    update = jnp.dot(
        features.reshape(part_count, -1), w_out.astype(jnp.float32), precision=highest
    )
    hidden = my_single.astype(jnp.float32) + update
    row_mean = jnp.mean(hidden, axis=1, keepdims=True)
    row_var = jnp.mean((hidden - row_mean) ** 2, axis=1, keepdims=True)
    rows = ((hidden - row_mean) * lax.rsqrt(row_var + norm_eps) * ln_gain[None, :]).astype(
        jnp.bfloat16
    )
    spread_rows = jnp.broadcast_to(rows[None], (n_col,) + rows.shape)
    single_out = lax.all_to_all(spread_rows, "col", 0, 0, tiled=False).reshape(row_count, width)
    return (pair_out, single_out)


def solution(mesh):
    return jax.shard_map(
        per_device,
        mesh=mesh,
        in_specs=(
            P(None, "row", "col"),
            P(),
            P(),
            P("col", None),
            P(None, "col"),
            P(None, "col"),
            P("col"),
            P("col"),
            P(),
            P(),
            P(),
            P(),
            P(),
            P(),
            P(),
            P(),
            P(),
            P(),
        ),
        out_specs=(P(None, "row", "col"), P("row", None)),
        check_vma=False,
    )
```

```python
import math

import jax
import jax.numpy as jnp
import numpy as np
from jax import lax
from jax.experimental import pallas as pl
from jax.experimental.pallas import tpu as pltpu
from jax.sharding import PartitionSpec as P

DILATION_STEP = 8


logit_scale = math.sqrt(1.0 / 3.0)
mask_penalty = 10000.0
norm_eps = 1e-05
highest = lax.Precision.HIGHEST


def edge_cells(rows):
    head = jnp.concatenate([row[:, :DILATION_STEP] for row in rows], axis=1)
    tail = jnp.concatenate([row[:, row.shape[1] - DILATION_STEP :] for row in rows], axis=1)
    return head, tail


def turn_kernel(pair_ref, rows_ref, head_ref, tail_ref):
    turned = jnp.swapaxes(pair_ref[...], 0, 1)
    rows_ref[...] = turned
    for block in range(turned.shape[0] // 8):
        head, tail = edge_cells([turned[8 * block + i] for i in range(8)])
        head_ref[block] = head
        tail_ref[block] = tail


def turn(pair):
    channels, row_count, col_count = pair.shape
    step = 16
    edge = jax.ShapeDtypeStruct((row_count // 8, channels, 64), pair.dtype)
    return pl.pallas_call(
        turn_kernel,
        grid=(row_count // step,),
        in_specs=[pl.BlockSpec((channels, step, col_count), lambda b: (0, b, 0))],
        out_specs=[
            pl.BlockSpec((step, channels, col_count), lambda b: (b, 0, 0)),
            pl.BlockSpec((step // 8, channels, 64), lambda b: (b, 0, 0)),
            pl.BlockSpec((step // 8, channels, 64), lambda b: (b, 0, 0)),
        ],
        out_shape=[
            jax.ShapeDtypeStruct((row_count, channels, col_count), pair.dtype),
            edge,
            edge,
        ],
        name="turn",
    )(pair)


def rim_kernel(up_ref, down_ref, head_ref, tail_ref):
    for index, ref in enumerate((up_ref, down_ref)):
        head, tail = edge_cells([ref[i] for i in range(8)])
        head_ref[index] = head
        tail_ref[index] = tail


def rim(up, down):
    edge = jax.ShapeDtypeStruct((2, up.shape[1], 64), up.dtype)
    return pl.pallas_call(rim_kernel, out_shape=[edge, edge], name="rim")(up, down)


def main_kernel(
    up_ref,
    own_ref,
    down_ref,
    left_ref,
    right_ref,
    weight_ref,
    bias_ref,
    head_bias_ref,
    base_ref,
    value_ref,
    owner_ref,
    out_ref,
    sums_ref,
    window_ref,
    soft_ref,
):
    step = pl.program_id(0)
    last = pl.num_programs(0) - 1
    channels = own_ref.shape[1]
    cols = own_ref.shape[2]
    slot = lax.rem(step, 3)

    def stage(source):
        for i in range(8):
            cells = source[i]
            cut = slice(8 * i, 8 * i + 8)
            window_ref[slot, i, 0:channels] = jnp.concatenate(
                [left_ref[0][:, cut], cells[:, : cols - 8]], axis=1
            )
            window_ref[slot, i, channels : 2 * channels] = cells
            window_ref[slot, i, 2 * channels : 3 * channels] = jnp.concatenate(
                [cells[:, 8:], right_ref[0][:, cut]], axis=1
            )

    @pl.when(step == 0)
    def _():
        stage(up_ref)

    @pl.when(jnp.logical_and(step > 0, step < last))
    def _():
        stage(own_ref)

    @pl.when(step == last)
    def _():
        stage(down_ref)

    @pl.when(step >= 2)
    def _():
        first = lax.rem(step + 1, 3)
        middle = lax.rem(step + 2, 3)
        lane = lax.broadcasted_iota(jnp.int32, (16, 128), 1)
        for i in range(8):
            conv = (
                jnp.dot(weight_ref[0], window_ref[first, i], preferred_element_type=jnp.float32)
                + jnp.dot(weight_ref[1], window_ref[middle, i], preferred_element_type=jnp.float32)
                + jnp.dot(weight_ref[2], window_ref[slot, i], preferred_element_type=jnp.float32)
            )
            conv = conv + bias_ref[...]
            bent = jnp.where(conv > 0.0, conv, jnp.exp(jnp.minimum(conv, 0.0)) - 1.0)
            cells = window_ref[middle, i, channels : 2 * channels].astype(jnp.float32)
            updated = (cells + bent).astype(jnp.bfloat16)
            out_ref[i] = updated
            bias = jnp.dot(head_bias_ref[...], updated, preferred_element_type=jnp.float32)
            logits = base_ref[i] + logit_scale * bias
            peak = jnp.max(logits, axis=1, keepdims=True)
            weights = jnp.exp(logits - peak).astype(jnp.bfloat16)
            total = jnp.sum(weights.astype(jnp.float32), axis=1, keepdims=True)
            pair_sum = lax.dot_general(
                weights, updated, (((1,), (1,)), ((), ())), preferred_element_type=jnp.float32
            )
            padded = jnp.concatenate([pair_sum, jnp.zeros((16, 64), jnp.float32)], axis=1)
            padded = jnp.where(lane == 104, peak, jnp.where(lane == 105, total, padded))
            row = (step - 2) * 8 + i
            sums_ref[row] = padded
            soft_ref[pl.ds(pl.multiple_of(row * 16, 16), 16), :] = weights

    @pl.when(step == last)
    def _():
        chunk = 256
        sub = lax.broadcasted_iota(jnp.int32, (chunk // 16, 16, 128), 1)
        for part in range(soft_ref.shape[0] // chunk):
            soft = soft_ref[part * chunk : (part + 1) * chunk, :]
            acc = jnp.dot(soft, value_ref[0], preferred_element_type=jnp.float32) + jnp.dot(
                soft, value_ref[1], preferred_element_type=jnp.float32
            )
            acc = acc.reshape(chunk // 16, 16, 512) * owner_ref[...][None]
            folded = jnp.sum(acc, axis=1, keepdims=True)
            rows = slice(part * chunk // 16, (part + 1) * chunk // 16)
            kept = sums_ref[rows]
            for k in range(4):
                lanes = folded[:, :, 128 * k : 128 * k + 128]
                kept = jnp.where(sub == 12 + k, lanes, kept)
            sums_ref[rows] = kept


def main(up, own, down, left, right, weight, bias, head_bias, base, value, owner):
    row_count, channels, col_count = own.shape
    steps = row_count // 8 + 2
    fixed3 = lambda b: (0, 0, 0)
    fixed2 = lambda b: (0, 0)
    late = lambda b: (jnp.maximum(b - 2, 0), 0, 0)
    return pl.pallas_call(
        main_kernel,
        grid=(steps,),
        in_specs=[
            pl.BlockSpec(up.shape, fixed3),
            pl.BlockSpec((8, channels, col_count), lambda b: (jnp.clip(b - 1, 0, steps - 3), 0, 0)),
            pl.BlockSpec(down.shape, fixed3),
            pl.BlockSpec((1, channels, 64), lambda b: (b, 0, 0)),
            pl.BlockSpec((1, channels, 64), lambda b: (b, 0, 0)),
            pl.BlockSpec(weight.shape, fixed3),
            pl.BlockSpec(bias.shape, fixed2),
            pl.BlockSpec(head_bias.shape, fixed2),
            pl.BlockSpec((8, 16, col_count), late),
            pl.BlockSpec(value.shape, fixed3),
            pl.BlockSpec(owner.shape, fixed2),
        ],
        out_specs=[
            pl.BlockSpec((8, channels, col_count), late),
            pl.BlockSpec((row_count, 16, 128), fixed3),
        ],
        out_shape=[
            jax.ShapeDtypeStruct((row_count, channels, col_count), jnp.bfloat16),
            jax.ShapeDtypeStruct((row_count, 16, 128), jnp.float32),
        ],
        scratch_shapes=[
            pltpu.VMEM((3, 8, 3 * channels, col_count), jnp.bfloat16),
            pltpu.VMEM((row_count * 16, col_count), jnp.bfloat16),
        ],
        name="main",
    )(up, own, down, left, right, weight, bias, head_bias, base, value, owner)


def in_pieces(value, count):
    parts = []
    for _ in range(count - 1):
        part = value.astype(jnp.bfloat16)
        parts.append(part)
        value = value - part.astype(jnp.float32)
    parts.append(value.astype(jnp.bfloat16))
    return parts


def dot32(a, b):
    return jnp.dot(a, b, preferred_element_type=jnp.float32)


def dot32_nt(a, b):
    return lax.dot_general(a, b, (((1,), (1,)), ((), ())), preferred_element_type=jnp.float32)


def to_global(local, frame):
    span = local.shape[1] // 3
    turned = []
    for x in range(3):
        total = frame[:, 9 + x : 10 + x]
        for d in range(3):
            column = frame[:, 3 * x + d : 3 * x + d + 1]
            total = total + column * local[:, span * d : span * (d + 1)]
        turned.append(total)
    return jnp.concatenate(turned, axis=1)


def keys_kernel(
    single_ref,
    w_key_ref,
    w_value_ref,
    w_kvpts_ref,
    frame_ref,
    pick_key_ref,
    pick_value_ref,
    shift_value_ref,
    points_ref,
    value_ref,
    key_ref,
    key_sq_ref,
):
    rows = single_ref[...]
    key = dot32(rows, w_key_ref[...])
    value = dot32(rows, w_value_ref[...]).astype(jnp.bfloat16)
    points = to_global(dot32(rows, w_kvpts_ref[...]), frame_ref[...])
    point_parts = in_pieces(points, 3)
    key_parts = in_pieces(
        jnp.concatenate([key, jnp.zeros((key.shape[0], 256 - key.shape[1]), jnp.float32)], axis=1), 3
    )
    whole = jnp.zeros((rows.shape[0], 256), jnp.float32)
    for index in range(3):
        picked = dot32(point_parts[index], pick_key_ref[...])
        whole = whole + picked
        key_ref[index, :, 0:256] = key_parts[index]
        key_ref[index, :, 256:512] = picked.astype(jnp.bfloat16)
    square = jnp.zeros((16, rows.shape[0]), jnp.float32)
    for part in in_pieces(whole * whole, 3):
        square = square + dot32_nt(points_ref[...], part)
    key_sq_ref[...] = square
    value_ref[0] = (
        dot32(value, shift_value_ref[...]) + dot32(point_parts[0], pick_value_ref[...])
    ).astype(jnp.bfloat16)
    value_ref[1] = dot32(point_parts[1], pick_value_ref[...]).astype(jnp.bfloat16)


def keys(single, w_key, w_value, w_kvpts, frame, pick_key, pick_value, shift_value, points):
    count = single.shape[0]
    return pl.pallas_call(
        keys_kernel,
        out_shape=[
            jax.ShapeDtypeStruct((2, count, 512), jnp.bfloat16),
            jax.ShapeDtypeStruct((3, count, 512), jnp.bfloat16),
            jax.ShapeDtypeStruct((16, count), jnp.float32),
        ],
        name="keys",
    )(single, w_key, w_value, w_kvpts, frame, pick_key, pick_value, shift_value, points)


def base_kernel(
    query_ref,
    w_query_ref,
    w_qpts_ref,
    frame_ref,
    key_ref,
    key_sq_ref,
    factor_ref,
    column_ref,
    key_row_ref,
    base_ref,
):
    rows = query_ref[...]
    count = rows.shape[0]
    query = dot32(rows, w_query_ref[...])
    points = to_global(dot32(rows, w_qpts_ref[...]), frame_ref[...])
    points = jnp.concatenate([points, jnp.zeros((count, 256 - points.shape[1]), jnp.float32)], axis=1)
    query = jnp.concatenate([query, jnp.zeros((count, 256 - query.shape[1]), jnp.float32)], axis=1)
    factor = factor_ref[...]
    query = query[:, None, :] * factor[None, :, 0:256]
    scaled = points[:, None, :] * factor[None, :, 256:512]
    own_sq = 0.5 * jnp.sum(scaled * points[:, None, :], axis=2, keepdims=True)
    query_parts = in_pieces(query.reshape(count * 16, 256), 3)
    point_parts = in_pieces(scaled.reshape(count * 16, 256), 3)
    total = jnp.zeros((count * 16, key_ref.shape[1]), jnp.float32)
    for a, b in ((2, 0), (1, 1), (0, 2), (1, 0), (0, 1), (0, 0)):
        total = total + dot32_nt(
            jnp.concatenate([query_parts[a], point_parts[a]], axis=1), key_ref[b]
        )
    scale = column_ref[:, 0:1]
    chain = column_ref[:, 1:2]
    same = (frame_ref[:, 12:13] == key_row_ref[0:1, :]).astype(jnp.float32)
    shared = scale * key_sq_ref[...]
    base_ref[...] = (
        total.reshape(count, 16, -1)
        - own_sq
        - shared[None]
        + chain[None] * same[:, None, :]
        - key_row_ref[1:2, :][None]
    )


def base_logits(query, w_query, w_qpts, frame, key, key_sq, factor, column, key_row):
    count = query.shape[0]
    step = 16
    whole2 = lambda b: (0, 0)
    whole3 = lambda b: (0, 0, 0)
    part = lambda b: (b, 0)
    return pl.pallas_call(
        base_kernel,
        grid=(count // step,),
        in_specs=[
            pl.BlockSpec((step, query.shape[1]), part),
            pl.BlockSpec(w_query.shape, whole2),
            pl.BlockSpec(w_qpts.shape, whole2),
            pl.BlockSpec((step, frame.shape[1]), part),
            pl.BlockSpec(key.shape, whole3),
            pl.BlockSpec(key_sq.shape, whole2),
            pl.BlockSpec(factor.shape, whole2),
            pl.BlockSpec(column.shape, whole2),
            pl.BlockSpec(key_row.shape, whole2),
        ],
        out_specs=pl.BlockSpec((step, 16, key.shape[1]), whole3_at),
        out_shape=jax.ShapeDtypeStruct((count, 16, key.shape[1]), jnp.float32),
        name="base",
    )(query, w_query, w_qpts, frame, key, key_sq, factor, column, key_row)


def whole3_at(b):
    return (b, 0, 0)


def finish_kernel(
    sums_ref, owner_ref, frame_ref, single_ref, w_pair_ref, w_flat_ref, gain_ref, out_ref
):
    sums = sums_ref[...]
    parts, count = sums.shape[0], sums.shape[1]
    width = single_ref.shape[1]
    live = lax.broadcasted_iota(jnp.int32, sums.shape[:3] + (1,), 2) < 12
    peaks = jnp.where(live, sums[:, :, :, 104:105], 0.0)
    scales = jnp.exp(peaks - jnp.max(peaks, axis=0, keepdims=True))
    counts = jnp.where(live, sums[:, :, :, 105:106], 1.0)
    totals = jnp.sum(counts * scales, axis=0, keepdims=True)
    scales = scales / totals
    means = jnp.sum(sums * scales, axis=0)
    flats = []
    for k in range(4):
        own = owner_ref[:, 128 * k : 128 * k + 128]
        lanes = jnp.sum(scales * own[None, None], axis=2)
        flats.append(jnp.sum(sums[:, :, 12 + k, :] * lanes, axis=0))
    flat = jnp.concatenate(flats, axis=1)
    frame = frame_ref[...]
    centred = [flat[:, 192 + 96 * x : 288 + 96 * x] - frame[:, 9 + x : 10 + x] for x in range(3)]
    local = [
        sum(frame[:, 3 * x + d : 3 * x + d + 1] * centred[x] for x in range(3)) for d in range(3)
    ]
    flat = jnp.concatenate([flat[:, :192]] + local, axis=1)
    paired = jnp.concatenate([means[:, h, 0:64] for h in range(12)], axis=1)
    update = jnp.zeros((count, width), jnp.float32)
    for values, weights in ((paired, w_pair_ref), (flat, w_flat_ref)):
        for part in reversed(in_pieces(values, 3)):
            update = update + dot32(part, weights[...])
    hidden = single_ref[...].astype(jnp.float32) + update
    row_mean = jnp.mean(hidden, axis=1, keepdims=True)
    row_var = jnp.mean((hidden - row_mean) ** 2, axis=1, keepdims=True)
    rows = ((hidden - row_mean) * lax.rsqrt(row_var + norm_eps) * gain_ref[...]).astype(jnp.bfloat16)
    for index in range(parts):
        out_ref[index] = rows


def finish(sums, owner, frame, single, w_pair, w_flat, gain):
    parts, count = sums.shape[:2]
    return pl.pallas_call(
        finish_kernel,
        out_shape=jax.ShapeDtypeStruct((parts, count, single.shape[1]), jnp.bfloat16),
        name="finish",
    )(sums, owner, frame, single, w_pair, w_flat, gain)


def frame_columns(quat_vec, trans, chain):
    rows = jnp.concatenate([rotations(quat_vec).reshape(9, -1), trans, chain], axis=0)
    return jnp.pad(rows, ((0, 16 - rows.shape[0]), (0, 0))).T


def tables(head_count, head_dim, query_points, value_points):
    both = query_points + value_points
    span = 3 * head_count * both
    pick_key = np.zeros((span, 256), np.float32)
    pick_value = np.zeros((span, 512), np.float32)
    shift_value = np.zeros((head_count * head_dim, 512), np.float32)
    points = np.zeros((16, 256), np.float32)
    scalars = np.zeros((16, 256), np.float32)
    owner = np.zeros((16, 512), np.float32)
    for h in range(head_count):
        for d in range(head_dim):
            lane = h * head_dim + d
            scalars[h, lane] = 1.0
            owner[h, lane] = 1.0
            shift_value[lane, lane] = 1.0
        for x in range(3):
            first = (x * head_count + h) * both
            for p in range(query_points):
                lane = (x * head_count + h) * query_points + p
                pick_key[first + p, lane] = 1.0
                points[h, lane] = 1.0
            for p in range(value_points):
                lane = head_count * head_dim + (x * head_count + h) * value_points + p
                pick_value[first + query_points + p, lane] = 1.0
                owner[h, lane] = 1.0
    return pick_key, pick_value, shift_value, points, scalars, owner


def shifted(cells, axis, forward):
    count = lax.axis_size(axis)
    if forward:
        routes = [(i, i + 1) for i in range(count - 1)]
    else:
        routes = [(i + 1, i) for i in range(count - 1)]
    return lax.ppermute(cells, axis, routes)


def ring(a, b, size):
    return min((a - b) % size, (b - a) % size)


def place(row, col, n_row, n_col):
    z_count = max(n_row // 4, 1)
    y_count = max(n_col // 2, 1)
    return (row // (2 * z_count) * 2 + col // y_count, col % y_count, row // 2 % z_count)


def query_routes(n_row, n_col):
    group = n_row // n_col
    z_count = max(n_row // 4, 1)
    y_count = max(n_col // 2, 1)
    pairs, offsets = [], np.zeros((n_row, n_col), np.int32)
    for holder_col in range(n_col):
        targets = [(holder_col * group + a, c) for a in range(group) for c in range(n_col)]
        sources = list(range(n_row))
        cost = np.zeros((n_row, n_row))
        for a, (row, col) in enumerate(targets):
            there = place(row, col, n_row, n_col)
            for b in sources:
                here = place(b, holder_col, n_row, n_col)
                hops = (
                    ring(there[0], here[0], 4)
                    + ring(there[1], here[1], y_count)
                    + ring(there[2], here[2], z_count)
                )
                cost[a, b] = float(hops) ** 4
        chosen = list(range(n_row))
        changed = True
        while changed:
            changed = False
            for a in range(n_row):
                for b in range(a):
                    now = cost[a, chosen[a]] + cost[b, chosen[b]]
                    then = cost[a, chosen[b]] + cost[b, chosen[a]]
                    if then < now - 1e-9:
                        chosen[a], chosen[b] = chosen[b], chosen[a]
                        changed = True
        for a, (row, col) in enumerate(targets):
            pairs.append((chosen[a] * n_col + holder_col, row * n_col + col))
            offsets[chosen[a], holder_col] = row % group
    return pairs, offsets


def pieces(value, count):
    parts = []
    for _ in range(count - 1):
        part = lax.reduce_precision(value, 8, 7)
        parts.append(part.astype(jnp.bfloat16))
        value = value - part
    parts.append(value.astype(jnp.bfloat16))
    return parts


def rotations(quat_vec):
    comp_b = quat_vec[0]
    comp_c = quat_vec[1]
    comp_d = quat_vec[2]
    inverse_norm = 1.0 / (1.0 + comp_b * comp_b + comp_c * comp_c + comp_d * comp_d)
    first_row = jnp.stack(
        [
            1.0 + comp_b * comp_b - comp_c * comp_c - comp_d * comp_d,
            2.0 * (comp_b * comp_c - comp_d),
            2.0 * (comp_b * comp_d + comp_c),
        ]
    )
    second_row = jnp.stack(
        [
            2.0 * (comp_b * comp_c + comp_d),
            1.0 - comp_b * comp_b + comp_c * comp_c - comp_d * comp_d,
            2.0 * (comp_c * comp_d - comp_b),
        ]
    )
    third_row = jnp.stack(
        [
            2.0 * (comp_b * comp_d - comp_c),
            2.0 * (comp_c * comp_d + comp_b),
            1.0 - comp_b * comp_b - comp_c * comp_c + comp_d * comp_d,
        ]
    )
    return jnp.stack([first_row, second_row, third_row]) * inverse_norm


def per_device(
    pair,
    conv_weight,
    conv_bias,
    single,
    quat_vec,
    trans,
    chain_id,
    residue_mask,
    w_query,
    w_key,
    w_value,
    w_qpts,
    w_kvpts,
    w_bias,
    head_weight,
    chain_weight,
    w_out,
    ln_gain,
):
    channels, row_count, col_count = pair.shape
    head_count = w_bias.shape[0]
    head_dim = w_query.shape[1] // head_count
    width = single.shape[1]
    query_points = w_qpts.shape[1] // (3 * head_count)
    value_points = w_kvpts.shape[1] // (3 * head_count) - query_points
    n_row, n_col = lax.axis_size("row"), lax.axis_size("col")
    part_count = row_count // n_col

    routes, offsets = query_routes(n_row, n_col)
    packed = jnp.concatenate([quat_vec, trans, chain_id.astype(jnp.float32)[None, :]], axis=0)
    offset = jnp.asarray(offsets)[lax.axis_index("row"), lax.axis_index("col")] * row_count
    mine_single = lax.dynamic_slice_in_dim(single, offset, row_count, 0)
    mine_frames = lax.dynamic_slice_in_dim(packed, offset, row_count, 1)
    frame_rows = jnp.concatenate(pieces(mine_frames, 3), axis=0)
    message = jnp.concatenate(
        [mine_single, jnp.pad(frame_rows, ((0, 3), (0, width - row_count)))], axis=0
    )
    message = lax.ppermute(message, ("row", "col"), routes)
    query_single = message[:row_count]
    frame_rows = message[row_count : row_count + 21, :row_count].astype(jnp.float32)
    query_frames = frame_rows[0:7] + frame_rows[7:14] + frame_rows[14:21]

    own, own_head, own_tail = turn(pair)
    up = shifted(own[row_count - DILATION_STEP :], "row", True)
    down = shifted(own[:DILATION_STEP], "row", False)
    rim_head, rim_tail = rim(up, down)
    left = shifted(
        jnp.concatenate([rim_tail[:1], own_tail, rim_tail[1:]], axis=0), "col", True
    )
    right = shifted(
        jnp.concatenate([rim_head[:1], own_head, rim_head[1:]], axis=0), "col", False
    )
    pick_key, pick_value, shift_value, points, scalars, owner = tables(
        head_count, head_dim, query_points, value_points
    )
    chain = chain_id.astype(jnp.float32)[None, :]
    present = residue_mask.astype(jnp.float32)
    value, key, key_sq = keys(
        single,
        w_key,
        w_value,
        w_kvpts,
        frame_columns(quat_vec, trans, chain),
        jnp.asarray(pick_key, jnp.bfloat16),
        jnp.asarray(pick_value, jnp.bfloat16),
        jnp.asarray(shift_value, jnp.bfloat16),
        jnp.asarray(points, jnp.bfloat16),
    )
    query_frame = frame_columns(query_frames[0:3], query_frames[3:6], query_frames[6:7])
    point_scale = logit_scale * jax.nn.softplus(head_weight) * math.sqrt(2.0 / (9.0 * query_points))
    head_pad = (0, 16 - head_count)
    column = jnp.stack(
        [jnp.pad(0.5 * point_scale, head_pad), jnp.pad(chain_weight, head_pad)], axis=1
    )
    factor = jnp.concatenate(
        [
            jnp.asarray(scalars * (logit_scale / math.sqrt(head_dim)), jnp.float32),
            jnp.asarray(points, jnp.float32) * jnp.pad(point_scale, head_pad)[:, None],
        ],
        axis=1,
    )
    key_row = jnp.concatenate([chain, mask_penalty * (1.0 - present)[None, :]], axis=0)
    base = base_logits(
        query_single,
        w_query,
        w_qpts,
        query_frame,
        key,
        key_sq,
        factor,
        column,
        key_row,
    )
    owner = jnp.asarray(owner, jnp.float32)
    weight = (
        conv_weight.reshape(3, 3, channels, channels)
        .transpose(0, 2, 1, 3)
        .reshape(3, channels, 3 * channels)
    )
    updated, sums = main(
        up,
        own,
        down,
        left,
        right,
        weight,
        conv_bias[:, None],
        jnp.pad(w_bias, ((0, 16 - head_count), (0, 0))),
        base,
        value,
        owner,
    )
    pair_out = updated.transpose(1, 0, 2)
    sums = sums.reshape(n_col, part_count, 16, 128)
    sums = lax.all_to_all(sums, "col", 0, 0, tiled=False)
    start = lax.axis_index("col") * part_count
    my_frame = lax.dynamic_slice_in_dim(query_frame, start, part_count, 0)
    my_single = lax.dynamic_slice_in_dim(query_single, start, part_count, 0)
    split_out = w_out.reshape(head_count, -1, width)
    w_flat = jnp.concatenate(
        [
            split_out[:, :head_dim].reshape(-1, width),
            split_out[:, head_dim + channels :]
            .reshape(head_count, 3, value_points, width)
            .transpose(1, 0, 2, 3)
            .reshape(-1, width),
        ],
        axis=0,
    )
    w_pair = split_out[:, head_dim : head_dim + channels].reshape(-1, width)
    spread_rows = finish(
        sums, owner, my_frame, my_single, w_pair, w_flat, ln_gain[None, :]
    )
    single_out = lax.all_to_all(spread_rows, "col", 0, 0, tiled=False).reshape(row_count, width)
    return (pair_out, single_out)


def solution(mesh):
    return jax.shard_map(
        per_device,
        mesh=mesh,
        in_specs=(
            P(None, "row", "col"),
            P(),
            P(),
            P("col", None),
            P(None, "col"),
            P(None, "col"),
            P("col"),
            P("col"),
            P(),
            P(),
            P(),
            P(),
            P(),
            P(),
            P(),
            P(),
            P(),
            P(),
        ),
        out_specs=(P(None, "row", "col"), P("row", None)),
        check_vma=False,
    )
```

```python
import math

import jax
import jax.numpy as jnp
import numpy as np
from jax import lax
from jax.experimental import pallas as pl
from jax.experimental.pallas import tpu as pltpu
from jax.sharding import PartitionSpec as P

DILATION_STEP = 8


logit_scale = math.sqrt(1.0 / 3.0)
mask_penalty = 10000.0
norm_eps = 1e-05
highest = lax.Precision.HIGHEST


def in_pieces(value, count):
    parts = []
    for _ in range(count - 1):
        part = value.astype(jnp.bfloat16)
        parts.append(part)
        value = value - part.astype(jnp.float32)
    parts.append(value.astype(jnp.bfloat16))
    return parts


def dot32(a, b):
    return jnp.dot(a, b, preferred_element_type=jnp.float32)


def dot32_nt(a, b):
    return lax.dot_general(a, b, (((1,), (1,)), ((), ())), preferred_element_type=jnp.float32)


def edge_cells(rows):
    head = jnp.concatenate([row[:, :DILATION_STEP] for row in rows], axis=1)
    tail = jnp.concatenate([row[:, row.shape[1] - DILATION_STEP :] for row in rows], axis=1)
    return head, tail


def turn_kernel(pair_ref, rows_ref, head_ref, tail_ref):
    turned = jnp.swapaxes(pair_ref[...], 0, 1)
    rows_ref[...] = turned
    for block in range(turned.shape[0] // 8):
        head, tail = edge_cells([turned[8 * block + i] for i in range(8)])
        head_ref[block] = head
        tail_ref[block] = tail


def turn(pair):
    channels, row_count, col_count = pair.shape
    step = 16
    edge = jax.ShapeDtypeStruct((row_count // 8, channels, 64), pair.dtype)
    return pl.pallas_call(
        turn_kernel,
        grid=(row_count // step,),
        in_specs=[pl.BlockSpec((channels, step, col_count), lambda b: (0, b, 0))],
        out_specs=[
            pl.BlockSpec((step, channels, col_count), lambda b: (b, 0, 0)),
            pl.BlockSpec((step // 8, channels, 64), lambda b: (b, 0, 0)),
            pl.BlockSpec((step // 8, channels, 64), lambda b: (b, 0, 0)),
        ],
        out_shape=[
            jax.ShapeDtypeStruct((row_count, channels, col_count), pair.dtype),
            edge,
            edge,
        ],
        name="turn",
    )(pair)


def rim_kernel(raw_up_ref, raw_down_ref, up_ref, down_ref, head_ref, tail_ref):
    for index, (raw, ref) in enumerate(((raw_up_ref, up_ref), (raw_down_ref, down_ref))):
        turned = jnp.swapaxes(raw[...], 0, 1)
        ref[...] = turned
        head, tail = edge_cells([turned[i] for i in range(8)])
        head_ref[index] = head
        tail_ref[index] = tail


def rim(raw_up, raw_down):
    channels, count, cols = raw_up.shape
    rows = jax.ShapeDtypeStruct((count, channels, cols), raw_up.dtype)
    edge = jax.ShapeDtypeStruct((2, channels, 64), raw_up.dtype)
    return pl.pallas_call(rim_kernel, out_shape=[rows, rows, edge, edge], name="rim")(
        raw_up, raw_down
    )


def as_column(row, count):
    shape = (count, row.shape[1])
    same = lax.broadcasted_iota(jnp.int32, shape, 0) == lax.broadcasted_iota(jnp.int32, shape, 1)
    return jnp.sum(jnp.where(same, row, 0.0), axis=1, keepdims=True)


def frame_columns(rows):
    comp_b, comp_c, comp_d = rows[0:1], rows[1:2], rows[2:3]
    bb, cc, dd = comp_b * comp_b, comp_c * comp_c, comp_d * comp_d
    inverse = 1.0 / (1.0 + bb + cc + dd)
    turned = [
        1.0 + bb - cc - dd,
        2.0 * (comp_b * comp_c - comp_d),
        2.0 * (comp_b * comp_d + comp_c),
        2.0 * (comp_b * comp_c + comp_d),
        1.0 - bb + cc - dd,
        2.0 * (comp_c * comp_d - comp_b),
        2.0 * (comp_b * comp_d - comp_c),
        2.0 * (comp_c * comp_d + comp_b),
        1.0 - bb - cc + dd,
    ]
    count = rows.shape[1]
    stacked = jnp.concatenate(
        [part * inverse for part in turned]
        + [rows[3:7], jnp.zeros((3, count), jnp.float32)],
        axis=0,
    )
    shape = (count, count)
    same = lax.broadcasted_iota(jnp.int32, shape, 0) == lax.broadcasted_iota(jnp.int32, shape, 1)
    eye = same.astype(jnp.bfloat16)
    columns = jnp.zeros((count, 16), jnp.float32)
    for part in in_pieces(stacked, 3):
        columns = columns + dot32_nt(eye, part)
    return columns


def main_kernel(
    up_ref,
    own_ref,
    down_ref,
    left_ref,
    right_ref,
    taps_ref,
    params_ref,
    raw_bias_ref,
    base_ref,
    value_ref,
    owner_ref,
    out_ref,
    sums_ref,
    window_ref,
    soft_ref,
    weight_ref,
    head_bias_ref,
    shift_ref,
):
    step = pl.program_id(0)
    last = pl.num_programs(0) - 1
    channels = own_ref.shape[1]
    cols = own_ref.shape[2]
    slot = lax.rem(step, 3)

    def stage(source):
        lane = lax.broadcasted_iota(jnp.int32, (channels, 128), 1)
        empty = jnp.zeros((channels, 64), jnp.bfloat16)
        before = jnp.concatenate([left_ref[0], empty], axis=1)
        after = jnp.concatenate([right_ref[0], empty], axis=1)
        top = channels
        for i in range(8):
            cells = source[i]
            ahead = [pltpu.roll(cells[:, 128 * k : 128 * k + 128], 8, 1) for k in range(2)]
            fill = pltpu.roll(before, (128 - 8 * i) % 128, 1)
            window_ref[slot, i, 0:top, 0:128] = jnp.where(lane < 8, fill, ahead[0])
            window_ref[slot, i, 0:top, 128:256] = jnp.where(lane < 8, ahead[0], ahead[1])
            window_ref[slot, i, top : 2 * top] = cells
            back = [pltpu.roll(cells[:, 128 * k : 128 * k + 128], 120, 1) for k in range(2)]
            fill = pltpu.roll(after, 120 - 8 * i, 1)
            window_ref[slot, i, 2 * top : 3 * top, 0:128] = jnp.where(lane >= 120, back[1], back[0])
            window_ref[slot, i, 2 * top : 3 * top, 128:256] = jnp.where(lane >= 120, fill, back[1])

    @pl.when(step == 0)
    def _():
        for dy in range(3):
            weight_ref[dy] = jnp.concatenate([taps_ref[3 * dy + dx] for dx in range(3)], axis=1)
        heads = raw_bias_ref.shape[0]
        pick = lax.broadcasted_iota(jnp.int32, (16, heads), 0) == lax.broadcasted_iota(
            jnp.int32, (16, heads), 1
        )
        head_bias_ref[...] = dot32(pick.astype(jnp.bfloat16), raw_bias_ref[...]).astype(jnp.bfloat16)
        shift_ref[...] = jnp.broadcast_to(as_column(params_ref[1:2, :], channels), (channels, cols))
        stage(up_ref)

    @pl.when(jnp.logical_and(step > 0, step < last))
    def _():
        stage(own_ref)

    @pl.when(step == last)
    def _():
        stage(down_ref)

    @pl.when(step >= 2)
    def _():
        first = lax.rem(step + 1, 3)
        middle = lax.rem(step + 2, 3)
        lane = lax.broadcasted_iota(jnp.int32, (8, 16, 128), 2)

        def convolve(i):
            return (
                jnp.dot(weight_ref[0], window_ref[first, i], preferred_element_type=jnp.float32)
                + jnp.dot(weight_ref[1], window_ref[middle, i], preferred_element_type=jnp.float32)
                + jnp.dot(weight_ref[2], window_ref[slot, i], preferred_element_type=jnp.float32)
            )

        shift = shift_ref[...]
        pending = convolve(0)
        for i in range(8):
            conv = pending + shift
            if i < 7:
                pending = convolve(i + 1)
            bent = jnp.where(conv > 0.0, conv, jnp.exp(jnp.minimum(conv, 0.0)) - 1.0)
            cells = window_ref[middle, i, channels : 2 * channels].astype(jnp.float32)
            out_ref[i] = (cells + bent).astype(jnp.bfloat16)
        bias = jnp.stack(
            [
                jnp.dot(head_bias_ref[...], out_ref[i], preferred_element_type=jnp.float32)
                for i in range(8)
            ]
        )
        logits = base_ref[...] + logit_scale * bias
        peak = jnp.max(logits, axis=2, keepdims=True)
        weights = jnp.exp(logits - peak).astype(jnp.bfloat16)
        total = jnp.sum(weights.astype(jnp.float32), axis=2, keepdims=True)
        pair_sum = jnp.stack(
            [
                lax.dot_general(
                    weights[i],
                    out_ref[i],
                    (((1,), (1,)), ((), ())),
                    preferred_element_type=jnp.float32,
                )
                for i in range(8)
            ]
        )
        padded = jnp.concatenate([pair_sum, jnp.zeros((8, 16, 64), jnp.float32)], axis=2)
        row = pl.multiple_of((step - 2) * 8, 8)
        sums_ref[pl.ds(row, 8)] = jnp.where(
            lane == 104, peak, jnp.where(lane == 105, total, padded)
        )
        soft_ref[pl.ds(pl.multiple_of(row * 16, 128), 128), :] = weights.reshape(128, cols)

    @pl.when(step == last)
    def _():
        chunk = 256
        sub = lax.broadcasted_iota(jnp.int32, (chunk // 16, 16, 128), 1)
        for part in range(soft_ref.shape[0] // chunk):
            soft = soft_ref[part * chunk : (part + 1) * chunk, :]
            acc = jnp.dot(soft, value_ref[0], preferred_element_type=jnp.float32) + jnp.dot(
                soft, value_ref[1], preferred_element_type=jnp.float32
            )
            acc = acc.reshape(chunk // 16, 16, 512) * owner_ref[...][None]
            folded = jnp.sum(acc, axis=1, keepdims=True)
            rows = slice(part * chunk // 16, (part + 1) * chunk // 16)
            kept = sums_ref[rows]
            for k in range(4):
                lanes = folded[:, :, 128 * k : 128 * k + 128]
                kept = jnp.where(sub == 12 + k, lanes, kept)
            sums_ref[rows] = kept


def main(up, own, down, left, right, weight, bias, head_bias, base, value, owner):
    row_count, channels, col_count = own.shape
    steps = row_count // 8 + 2
    fixed3 = lambda b: (0, 0, 0)
    fixed2 = lambda b: (0, 0)
    late = lambda b: (jnp.maximum(b - 2, 0), 0, 0)
    return pl.pallas_call(
        main_kernel,
        grid=(steps,),
        in_specs=[
            pl.BlockSpec(up.shape, fixed3),
            pl.BlockSpec((8, channels, col_count), lambda b: (jnp.clip(b - 1, 0, steps - 3), 0, 0)),
            pl.BlockSpec(down.shape, fixed3),
            pl.BlockSpec((1, channels, 64), lambda b: (b, 0, 0)),
            pl.BlockSpec((1, channels, 64), lambda b: (b, 0, 0)),
            pl.BlockSpec(weight.shape, fixed3),
            pl.BlockSpec(bias.shape, fixed2),
            pl.BlockSpec(head_bias.shape, fixed2),
            pl.BlockSpec((8, 16, col_count), late),
            pl.BlockSpec(value.shape, fixed3),
            pl.BlockSpec(owner.shape, fixed2),
        ],
        out_specs=[
            pl.BlockSpec((8, channels, col_count), late),
            pl.BlockSpec((row_count, 16, 128), fixed3),
        ],
        out_shape=[
            jax.ShapeDtypeStruct((row_count, channels, col_count), jnp.bfloat16),
            jax.ShapeDtypeStruct((row_count, 16, 128), jnp.float32),
        ],
        scratch_shapes=[
            pltpu.VMEM((3, 8, 3 * channels, col_count), jnp.bfloat16),
            pltpu.VMEM((row_count * 16, col_count), jnp.bfloat16),
            pltpu.VMEM((3, channels, 3 * channels), jnp.bfloat16),
            pltpu.VMEM((16, channels), jnp.bfloat16),
            pltpu.VMEM((channels, col_count), jnp.float32),
        ],
        name="main",
    )(up, own, down, left, right, weight, bias, head_bias, base, value, owner)


def to_global(local, frame):
    span = local.shape[1] // 3
    turned = []
    for x in range(3):
        total = frame[:, 9 + x : 10 + x]
        for d in range(3):
            column = frame[:, 3 * x + d : 3 * x + d + 1]
            total = total + column * local[:, span * d : span * (d + 1)]
        turned.append(total)
    return jnp.concatenate(turned, axis=1)


def keys_kernel(
    single_ref,
    w_key_ref,
    w_value_ref,
    w_kvpts_ref,
    frame_ref,
    pick_key_ref,
    pick_value_ref,
    shift_value_ref,
    points_ref,
    value_ref,
    key_ref,
    key_sq_ref,
):
    rows = single_ref[...]
    key = dot32_nt(rows, w_key_ref[...])
    value = dot32_nt(rows, w_value_ref[...]).astype(jnp.bfloat16)
    points = to_global(dot32_nt(rows, w_kvpts_ref[...]), frame_columns(frame_ref[...]))
    point_parts = in_pieces(points, 3)
    key_parts = in_pieces(
        jnp.concatenate([key, jnp.zeros((key.shape[0], 256 - key.shape[1]), jnp.float32)], axis=1), 3
    )
    whole = jnp.zeros((rows.shape[0], 256), jnp.float32)
    for index in range(3):
        picked = dot32(point_parts[index], pick_key_ref[...])
        whole = whole + picked
        key_ref[index, :, 0:256] = key_parts[index]
        key_ref[index, :, 256:512] = picked.astype(jnp.bfloat16)
    square = jnp.zeros((16, rows.shape[0]), jnp.float32)
    for part in in_pieces(whole * whole, 3):
        square = square + dot32_nt(points_ref[...], part)
    key_sq_ref[...] = square
    value_ref[0] = (
        dot32(value, shift_value_ref[...]) + dot32(point_parts[0], pick_value_ref[...])
    ).astype(jnp.bfloat16)
    value_ref[1] = dot32(point_parts[1], pick_value_ref[...]).astype(jnp.bfloat16)


def keys(single, w_key, w_value, w_kvpts, frame, pick_key, pick_value, shift_value, points):
    count = single.shape[0]
    return pl.pallas_call(
        keys_kernel,
        out_shape=[
            jax.ShapeDtypeStruct((2, count, 512), jnp.bfloat16),
            jax.ShapeDtypeStruct((3, count, 512), jnp.bfloat16),
            jax.ShapeDtypeStruct((16, count), jnp.float32),
        ],
        name="keys",
    )(single, w_key, w_value, w_kvpts, frame, pick_key, pick_value, shift_value, points)


def base_kernel(
    query_ref,
    w_query_ref,
    w_qpts_ref,
    key_ref,
    key_sq_ref,
    table_ref,
    params_ref,
    key_row_ref,
    base_ref,
    frame_ref,
):
    step = pl.program_id(0)
    count = base_ref.shape[0]

    @pl.when(step == 0)
    def _():
        every = query_ref.shape[0] - 24
        tail = query_ref[every:, 0:every].astype(jnp.float32)
        frame_ref[...] = frame_columns(tail[0:8] + tail[8:16] + tail[16:24])

    own = pl.ds(pl.multiple_of(step * count, count), count)
    rows = query_ref[own, :]
    frame = frame_ref[own, :]
    query = dot32_nt(rows, w_query_ref[...])
    points = to_global(dot32_nt(rows, w_qpts_ref[...]), frame)
    points = jnp.concatenate([points, jnp.zeros((count, 256 - points.shape[1]), jnp.float32)], axis=1)
    query = jnp.concatenate([query, jnp.zeros((count, 256 - query.shape[1]), jnp.float32)], axis=1)
    point_scale = as_column(params_ref[2:3, :], 16)
    query = query[:, None, :] * table_ref[:, 0:256][None]
    scaled = points[:, None, :] * (table_ref[:, 256:512] * point_scale)[None]
    own_sq = 0.5 * jnp.sum(scaled * points[:, None, :], axis=2, keepdims=True)
    query_parts = in_pieces(query.reshape(count * 16, 256), 3)
    point_parts = in_pieces(scaled.reshape(count * 16, 256), 3)
    total = jnp.zeros((count * 16, key_ref.shape[1]), jnp.float32)
    for a, b in ((2, 0), (1, 1), (0, 2), (1, 0), (0, 1), (0, 0)):
        total = total + dot32_nt(
            jnp.concatenate([query_parts[a], point_parts[a]], axis=1), key_ref[b]
        )
    scale = 0.5 * point_scale
    chain = as_column(params_ref[3:4, :], 16)
    same = (frame[:, 12:13] == key_row_ref[6:7, :]).astype(jnp.float32)
    shared = scale * key_sq_ref[...]
    base_ref[...] = (
        total.reshape(count, 16, -1)
        - own_sq
        - shared[None]
        + chain[None] * same[:, None, :]
        - key_row_ref[7:8, :][None]
    )


def base_logits(query, w_query, w_qpts, key, key_sq, table, params, key_row):
    count = query.shape[0] - 24
    step = 16
    whole2 = lambda b: (0, 0)
    whole3 = lambda b: (0, 0, 0)
    operands = (query, w_query, w_qpts, key, key_sq, table, params, key_row)
    return pl.pallas_call(
        base_kernel,
        grid=(count // step,),
        in_specs=[pl.BlockSpec(x.shape, whole3 if x.ndim == 3 else whole2) for x in operands],
        out_specs=[
            pl.BlockSpec((step, 16, key.shape[1]), whole3_at),
            pl.BlockSpec((count, 16), whole2),
        ],
        out_shape=[
            jax.ShapeDtypeStruct((count, 16, key.shape[1]), jnp.float32),
            jax.ShapeDtypeStruct((count, 16), jnp.float32),
        ],
        name="base",
    )(*operands)


def whole3_at(b):
    return (b, 0, 0)


def finish_kernel(
    sums_ref, owner_ref, frame_ref, message_ref, w_out_ref, params_ref, out_ref
):
    sums = sums_ref[...]
    parts, count = sums.shape[0], sums.shape[1]
    width = message_ref.shape[1]
    place = lax.axis_index("col") * count
    live = lax.broadcasted_iota(jnp.int32, sums.shape[:3] + (1,), 2) < 12
    peaks = jnp.where(live, sums[:, :, :, 104:105], 0.0)
    scales = jnp.exp(peaks - jnp.max(peaks, axis=0, keepdims=True))
    counts = jnp.where(live, sums[:, :, :, 105:106], 1.0)
    totals = jnp.sum(counts * scales, axis=0, keepdims=True)
    scales = scales / totals
    means = jnp.sum(sums * scales, axis=0)
    flats = []
    for k in range(4):
        own = owner_ref[:, 128 * k : 128 * k + 128]
        lanes = jnp.sum(scales * own[None, None], axis=2)
        flats.append(jnp.sum(sums[:, :, 12 + k, :] * lanes, axis=0))
    flat = jnp.concatenate(flats, axis=1)
    frame = frame_ref[pl.ds(pl.multiple_of(place, count), count), :]
    centred = [flat[:, 192 + 96 * x : 288 + 96 * x] - frame[:, 9 + x : 10 + x] for x in range(3)]
    local = [
        sum(frame[:, 3 * x + d : 3 * x + d + 1] * centred[x] for x in range(3)) for d in range(3)
    ]
    features = []
    for h in range(12):
        features += [flat[:, 16 * h : 16 * h + 16], means[:, h, 0:64]]
        features += [part[:, 8 * h : 8 * h + 8] for part in local]
    update = jnp.zeros((count, width), jnp.float32)
    for part in reversed(in_pieces(jnp.concatenate(features, axis=1), 3)):
        update = update + dot32(part, w_out_ref[...])
    shape = (count, message_ref.shape[0])
    mine = lax.broadcasted_iota(jnp.int32, shape, 1) == place + lax.broadcasted_iota(
        jnp.int32, shape, 0
    )
    single = dot32(mine.astype(jnp.bfloat16), message_ref[...])
    hidden = single + update
    row_mean = jnp.mean(hidden, axis=1, keepdims=True)
    row_var = jnp.mean((hidden - row_mean) ** 2, axis=1, keepdims=True)
    rows = ((hidden - row_mean) * lax.rsqrt(row_var + norm_eps) * params_ref[0:1, :]).astype(jnp.bfloat16)
    for index in range(parts):
        out_ref[index] = rows


def finish(sums, owner, frame, message, w_out, params):
    parts, count = sums.shape[:2]
    return pl.pallas_call(
        finish_kernel,
        out_shape=jax.ShapeDtypeStruct((parts, count, message.shape[1]), jnp.bfloat16),
        name="finish",
    )(sums, owner, frame, message, w_out, params)


def pack_kernel(single_ref, rows_ref, message_ref):
    count = message_ref.shape[0] - 24
    width = message_ref.shape[1]
    slots = single_ref.shape[0] // count
    slot = lax.axis_index("row") % slots
    message_ref[0:count, :] = single_ref[pl.ds(pl.multiple_of(slot * count, count), count), :]
    rows = rows_ref[:, 0:count]
    for k in range(1, slots):
        rows = jnp.where(slot == k, rows_ref[:, k * count : (k + 1) * count], rows)
    rows = jnp.concatenate([rows, jnp.zeros((rows.shape[0], width - count), jnp.float32)], axis=1)
    for k, part in enumerate(in_pieces(rows, 3)):
        message_ref[count + 8 * k : count + 8 * k + 8, :] = part


def pack(single, rows, count):
    return pl.pallas_call(
        pack_kernel,
        out_shape=jax.ShapeDtypeStruct((count + 24, single.shape[1]), single.dtype),
        name="pack",
    )(single, rows)


def tables(head_count, head_dim, query_points, value_points):
    both = query_points + value_points
    span = 3 * head_count * both
    pick_key = np.zeros((span, 256), np.float32)
    pick_value = np.zeros((span, 512), np.float32)
    shift_value = np.zeros((head_count * head_dim, 512), np.float32)
    points = np.zeros((16, 256), np.float32)
    scalars = np.zeros((16, 256), np.float32)
    owner = np.zeros((16, 512), np.float32)
    for h in range(head_count):
        for d in range(head_dim):
            lane = h * head_dim + d
            scalars[h, lane] = 1.0
            owner[h, lane] = 1.0
            shift_value[lane, lane] = 1.0
        for x in range(3):
            first = (x * head_count + h) * both
            for p in range(query_points):
                lane = (x * head_count + h) * query_points + p
                pick_key[first + p, lane] = 1.0
                points[h, lane] = 1.0
            for p in range(value_points):
                lane = head_count * head_dim + (x * head_count + h) * value_points + p
                pick_value[first + query_points + p, lane] = 1.0
                owner[h, lane] = 1.0
    return pick_key, pick_value, shift_value, points, scalars, owner


def shifted(cells, axis, forward):
    count = lax.axis_size(axis)
    if forward:
        routes = [(i, i + 1) for i in range(count - 1)]
    else:
        routes = [(i + 1, i) for i in range(count - 1)]
    return lax.ppermute(cells, axis, routes)


def query_routes(n_row, n_col):
    group = n_row // n_col
    pairs = []
    for holder_col in range(n_col):
        for holder in range(n_row):
            slot = holder // group
            half = n_col // 2
            col = slot // half * half + (slot + half // 2) % half
            target = holder_col * group + holder % group
            pairs.append((holder * n_col + holder_col, target * n_col + col))
    return pairs


def per_device(
    pair,
    conv_weight,
    conv_bias,
    single,
    quat_vec,
    trans,
    chain_id,
    residue_mask,
    w_query,
    w_key,
    w_value,
    w_qpts,
    w_kvpts,
    w_bias,
    head_weight,
    chain_weight,
    w_out,
    ln_gain,
):
    channels, row_count, col_count = pair.shape
    head_count = w_bias.shape[0]
    head_dim = w_query.shape[1] // head_count
    width = single.shape[1]
    query_points = w_qpts.shape[1] // (3 * head_count)
    value_points = w_kvpts.shape[1] // (3 * head_count) - query_points
    n_row, n_col = lax.axis_size("row"), lax.axis_size("col")
    part_count = row_count // n_col

    raw_up = shifted(pair[:, row_count - DILATION_STEP :], "row", True)
    raw_down = shifted(pair[:, :DILATION_STEP], "row", False)
    routes = query_routes(n_row, n_col)
    rows = jnp.concatenate(
        [
            quat_vec,
            trans,
            chain_id.astype(jnp.float32)[None, :],
            mask_penalty * (1.0 - residue_mask.astype(jnp.float32))[None, :],
        ],
        axis=0,
    )
    message = lax.ppermute(pack(single, rows, row_count), ("row", "col"), routes)
    point_scale = logit_scale * jax.nn.softplus(head_weight) * math.sqrt(2.0 / (9.0 * query_points))
    wide = lambda row: jnp.pad(row, (0, width - row.shape[0]))[None, :]
    params = jnp.concatenate(
        [wide(ln_gain), wide(conv_bias), wide(point_scale), wide(chain_weight)]
        + [jnp.zeros((4, width), jnp.float32)],
        axis=0,
    )
    own, own_head, own_tail = turn(pair)
    up, down, rim_head, rim_tail = rim(raw_up, raw_down)
    to_right = jnp.concatenate([rim_tail[:1], own_tail, rim_tail[1:]], axis=0)
    to_left = jnp.concatenate([rim_head[:1], own_head, rim_head[1:]], axis=0)
    to_right, to_left, key_rows = lax.optimization_barrier((to_right, to_left, rows))
    left = shifted(to_right, "col", True)
    right = shifted(to_left, "col", False)
    pick_key, pick_value, shift_value, points, scalars, owner = tables(
        head_count, head_dim, query_points, value_points
    )
    value, key, key_sq = keys(
        single,
        w_key.T,
        w_value.T,
        w_kvpts.T,
        key_rows,
        jnp.asarray(pick_key, jnp.bfloat16),
        jnp.asarray(pick_value, jnp.bfloat16),
        jnp.asarray(shift_value, jnp.bfloat16),
        jnp.asarray(points, jnp.bfloat16),
    )
    table = np.concatenate([scalars * (logit_scale / math.sqrt(head_dim)), points], axis=1)
    base, frame = base_logits(
        message,
        w_query.T,
        w_qpts.T,
        key,
        key_sq,
        jnp.asarray(table, jnp.float32),
        params,
        key_rows,
    )
    owner = jnp.asarray(owner, jnp.float32)
    updated, sums = main(
        up,
        own,
        down,
        left,
        right,
        conv_weight,
        params,
        w_bias,
        base,
        value,
        owner,
    )
    pair_out = updated.transpose(1, 0, 2)
    sums = sums.reshape(n_col, part_count, 16, 128)
    sums = lax.all_to_all(sums, "col", 0, 0, tiled=False)
    spread_rows = finish(sums, owner, frame, message, w_out, params)
    single_out = lax.all_to_all(spread_rows, "col", 0, 0, tiled=False).reshape(row_count, width)
    return (pair_out, single_out)


def solution(mesh):
    return jax.shard_map(
        per_device,
        mesh=mesh,
        in_specs=(
            P(None, "row", "col"),
            P(),
            P(),
            P("col", None),
            P(None, "col"),
            P(None, "col"),
            P("col"),
            P("col"),
            P(),
            P(),
            P(),
            P(),
            P(),
            P(),
            P(),
            P(),
            P(),
            P(),
        ),
        out_specs=(P(None, "row", "col"), P("row", None)),
        check_vma=False,
    )
```

```python
import math

import jax
import jax.numpy as jnp
import numpy as np
from jax import lax
from jax.experimental import pallas as pl
from jax.experimental.pallas import tpu as pltpu
from jax.sharding import PartitionSpec as P

DILATION_STEP = 8


logit_scale = math.sqrt(1.0 / 3.0)
mask_penalty = 10000.0
norm_eps = 1e-05
highest = lax.Precision.HIGHEST


def in_pieces(value, count):
    parts = []
    for _ in range(count - 1):
        part = value.astype(jnp.bfloat16)
        parts.append(part)
        value = value - part.astype(jnp.float32)
    parts.append(value.astype(jnp.bfloat16))
    return parts


def dot32(a, b):
    return jnp.dot(a, b, preferred_element_type=jnp.float32)


def dot32_nt(a, b):
    return lax.dot_general(a, b, (((1,), (1,)), ((), ())), preferred_element_type=jnp.float32)


def edge_cells(rows):
    head = jnp.concatenate([row[:, :DILATION_STEP] for row in rows], axis=1)
    tail = jnp.concatenate([row[:, row.shape[1] - DILATION_STEP :] for row in rows], axis=1)
    return head, tail


def turn_kernel(pair_ref, rows_ref, head_ref, tail_ref):
    turned = jnp.swapaxes(pair_ref[...], 0, 1)
    rows_ref[...] = turned
    for block in range(turned.shape[0] // 8):
        head, tail = edge_cells([turned[8 * block + i] for i in range(8)])
        head_ref[block] = head
        tail_ref[block] = tail


def turn(pair):
    channels, row_count, col_count = pair.shape
    step = 16
    edge = jax.ShapeDtypeStruct((row_count // 8, channels, 64), pair.dtype)
    return pl.pallas_call(
        turn_kernel,
        grid=(row_count // step,),
        in_specs=[pl.BlockSpec((channels, step, col_count), lambda b: (0, b, 0))],
        out_specs=[
            pl.BlockSpec((step, channels, col_count), lambda b: (b, 0, 0)),
            pl.BlockSpec((step // 8, channels, 64), lambda b: (b, 0, 0)),
            pl.BlockSpec((step // 8, channels, 64), lambda b: (b, 0, 0)),
        ],
        out_shape=[
            jax.ShapeDtypeStruct((row_count, channels, col_count), pair.dtype),
            edge,
            edge,
        ],
        name="turn",
    )(pair)


def rim_kernel(
    raw_up_ref,
    raw_down_ref,
    own_head_ref,
    own_tail_ref,
    up_ref,
    down_ref,
    to_left_ref,
    to_right_ref,
    near_ref,
    sems,
):
    copies = [
        pltpu.make_async_copy(raw, near_ref.at[k], sems.at[k])
        for k, raw in enumerate((raw_up_ref, raw_down_ref))
    ]
    for copy in copies:
        copy.start()
    inner = own_head_ref.shape[0]
    to_left_ref[1 : 1 + inner] = own_head_ref[...]
    to_right_ref[1 : 1 + inner] = own_tail_ref[...]
    for k, (ref, index) in enumerate(((up_ref, 0), (down_ref, inner + 1))):
        copies[k].wait()
        turned = jnp.swapaxes(near_ref[k], 0, 1)
        ref[...] = turned
        head, tail = edge_cells([turned[i] for i in range(8)])
        to_left_ref[index] = head
        to_right_ref[index] = tail


def rim(raw_up, raw_down, own_head, own_tail):
    channels, count, cols = raw_up.shape
    inner = own_head.shape[0]
    rows = jax.ShapeDtypeStruct((count, channels, cols), raw_up.dtype)
    edge = jax.ShapeDtypeStruct((inner + 2, channels, 64), raw_up.dtype)
    vmem = pl.BlockSpec(memory_space=pltpu.VMEM)
    return pl.pallas_call(
        rim_kernel,
        in_specs=[pl.BlockSpec(memory_space=pl.ANY)] * 2 + [vmem] * 2,
        out_specs=[vmem] * 4,
        out_shape=[rows, rows, edge, edge],
        scratch_shapes=[
            pltpu.VMEM((2, channels, count, cols), raw_up.dtype),
            pltpu.SemaphoreType.DMA((2,)),
        ],
        name="rim",
    )(raw_up, raw_down, own_head, own_tail)


def as_column(row, count):
    shape = (count, row.shape[1])
    same = lax.broadcasted_iota(jnp.int32, shape, 0) == lax.broadcasted_iota(jnp.int32, shape, 1)
    return jnp.sum(jnp.where(same, row, 0.0), axis=1, keepdims=True)


def frame_columns(rows):
    comp_b, comp_c, comp_d = rows[0:1], rows[1:2], rows[2:3]
    bb, cc, dd = comp_b * comp_b, comp_c * comp_c, comp_d * comp_d
    inverse = 1.0 / (1.0 + bb + cc + dd)
    turned = [
        1.0 + bb - cc - dd,
        2.0 * (comp_b * comp_c - comp_d),
        2.0 * (comp_b * comp_d + comp_c),
        2.0 * (comp_b * comp_c + comp_d),
        1.0 - bb + cc - dd,
        2.0 * (comp_c * comp_d - comp_b),
        2.0 * (comp_b * comp_d - comp_c),
        2.0 * (comp_c * comp_d + comp_b),
        1.0 - bb - cc + dd,
    ]
    count = rows.shape[1]
    stacked = jnp.concatenate(
        [part * inverse for part in turned]
        + [rows[3:7], jnp.zeros((3, count), jnp.float32)],
        axis=0,
    )
    shape = (count, count)
    same = lax.broadcasted_iota(jnp.int32, shape, 0) == lax.broadcasted_iota(jnp.int32, shape, 1)
    eye = same.astype(jnp.bfloat16)
    columns = jnp.zeros((count, 16), jnp.float32)
    for part in in_pieces(stacked, 3):
        columns = columns + dot32_nt(eye, part)
    return columns


def main_kernel(
    up_ref,
    own_ref,
    down_ref,
    left_ref,
    right_ref,
    taps_ref,
    params_ref,
    raw_bias_ref,
    base_ref,
    value_ref,
    owner_ref,
    out_ref,
    sums_ref,
    window_ref,
    soft_ref,
    weight_ref,
    head_bias_ref,
    shift_ref,
):
    step = pl.program_id(0)
    last = pl.num_programs(0) - 1
    channels = own_ref.shape[1]
    cols = own_ref.shape[2]
    slot = lax.rem(step, 4)

    def stage(picked=range(8)):
        lane = lax.broadcasted_iota(jnp.int32, (channels, 128), 1)
        empty = jnp.zeros((channels, 64), jnp.bfloat16)
        before = jnp.concatenate([left_ref[0], empty], axis=1)
        after = jnp.concatenate([right_ref[0], empty], axis=1)
        top = channels
        for i in picked:
            cells = jnp.where(
                step == 0, up_ref[i], jnp.where(step == last - 1, down_ref[i], own_ref[i])
            )
            ahead = [pltpu.roll(cells[:, 128 * k : 128 * k + 128], 8, 1) for k in range(2)]
            fill = pltpu.roll(before, (128 - 8 * i) % 128, 1)
            window_ref[slot, i, 0:top, 0:128] = jnp.where(lane < 8, fill, ahead[0])
            window_ref[slot, i, 0:top, 128:256] = jnp.where(lane < 8, ahead[0], ahead[1])
            window_ref[slot, i, top : 2 * top] = cells
            back = [pltpu.roll(cells[:, 128 * k : 128 * k + 128], 120, 1) for k in range(2)]
            fill = pltpu.roll(after, 120 - 8 * i, 1)
            window_ref[slot, i, 2 * top : 3 * top, 0:128] = jnp.where(lane >= 120, back[1], back[0])
            window_ref[slot, i, 2 * top : 3 * top, 128:256] = jnp.where(lane >= 120, fill, back[1])

    @pl.when(step == 0)
    def _():
        for dy in range(3):
            weight_ref[dy] = jnp.concatenate([taps_ref[3 * dy + dx] for dx in range(3)], axis=1)
        heads = raw_bias_ref.shape[0]
        pick = lax.broadcasted_iota(jnp.int32, (16, heads), 0) == lax.broadcasted_iota(
            jnp.int32, (16, heads), 1
        )
        head_bias_ref[...] = dot32(pick.astype(jnp.bfloat16), raw_bias_ref[...]).astype(jnp.bfloat16)
        shift_ref[...] = jnp.broadcast_to(as_column(params_ref[1:2, :], channels), (channels, cols))

    @pl.when(step < 3)
    def _():
        stage()

    @pl.when(step >= 3)
    def _():
        first = lax.rem(step + 1, 4)
        middle = lax.rem(step + 2, 4)
        third = lax.rem(step + 3, 4)
        lane = lax.broadcasted_iota(jnp.int32, (8, 16, 128), 2)

        def convolve(i):
            return (
                jnp.dot(weight_ref[0], window_ref[first, i], preferred_element_type=jnp.float32)
                + jnp.dot(weight_ref[1], window_ref[middle, i], preferred_element_type=jnp.float32)
                + jnp.dot(weight_ref[2], window_ref[third, i], preferred_element_type=jnp.float32)
            )

        shift = shift_ref[...]
        pending = convolve(0)
        for i in range(8):
            conv = pending + shift
            if i < 7:
                pending = convolve(i + 1)
            bent = jnp.where(conv > 0.0, conv, jnp.exp(jnp.minimum(conv, 0.0)) - 1.0)
            cells = window_ref[middle, i, channels : 2 * channels].astype(jnp.float32)
            out_ref[i] = (cells + bent).astype(jnp.bfloat16)
            stage((i,))
        bias = jnp.stack(
            [
                jnp.dot(head_bias_ref[...], out_ref[i], preferred_element_type=jnp.float32)
                for i in range(8)
            ]
        )
        logits = base_ref[...] + logit_scale * bias
        peak = jnp.max(logits, axis=2, keepdims=True)
        weights = jnp.exp(logits - peak).astype(jnp.bfloat16)
        total = jnp.sum(weights.astype(jnp.float32), axis=2, keepdims=True)
        pair_sum = jnp.stack(
            [
                lax.dot_general(
                    weights[i],
                    out_ref[i],
                    (((1,), (1,)), ((), ())),
                    preferred_element_type=jnp.float32,
                )
                for i in range(8)
            ]
        )
        padded = jnp.concatenate([pair_sum, jnp.zeros((8, 16, 64), jnp.float32)], axis=2)
        row = pl.multiple_of((step - 3) * 8, 8)
        sums_ref[pl.ds(row, 8)] = jnp.where(
            lane == 104, peak, jnp.where(lane == 105, total, padded)
        )
        soft_ref[pl.ds(pl.multiple_of(row * 16, 128), 128), :] = weights.reshape(128, cols)

    @pl.when(step == last)
    def _():
        chunk = 256
        sub = lax.broadcasted_iota(jnp.int32, (chunk // 16, 16, 128), 1)
        lane = lax.broadcasted_iota(jnp.int32, (chunk // 16, 16, 128), 2)
        for part in range(soft_ref.shape[0] // chunk):
            soft = soft_ref[part * chunk : (part + 1) * chunk, :]
            acc = jnp.dot(soft, value_ref[0], preferred_element_type=jnp.float32) + jnp.dot(
                soft, value_ref[1], preferred_element_type=jnp.float32
            )
            acc = acc.reshape(chunk // 16, 16, 512) * owner_ref[...][None]
            folded = jnp.sum(acc, axis=1, keepdims=True)
            rows = slice(part * chunk // 16, (part + 1) * chunk // 16)
            kept = sums_ref[rows]
            marks = jnp.where(
                lane == 96 + sub,
                kept[:, :, 104:105],
                jnp.where(lane == 108 + sub, kept[:, :, 105:106], 0.0),
            )
            marks = jnp.sum(jnp.where(sub < 12, marks, 0.0), axis=1, keepdims=True)
            for k in range(4):
                lanes = folded[:, :, 128 * k : 128 * k + 128]
                if k == 3:
                    lanes = lanes + marks
                kept = jnp.where(sub == 12 + k, lanes, kept)
            sums_ref[rows] = kept


def main(up, own, down, left, right, weight, bias, head_bias, base, value, owner):
    row_count, channels, col_count = own.shape
    steps = row_count // 8 + 3
    fixed3 = lambda b: (0, 0, 0)
    fixed2 = lambda b: (0, 0)
    late = lambda b: (jnp.maximum(b - 3, 0), 0, 0)
    return pl.pallas_call(
        main_kernel,
        grid=(steps,),
        in_specs=[
            pl.BlockSpec(up.shape, fixed3),
            pl.BlockSpec((8, channels, col_count), lambda b: (jnp.clip(b - 1, 0, steps - 4), 0, 0)),
            pl.BlockSpec(down.shape, fixed3),
            pl.BlockSpec((1, channels, 64), lambda b: (jnp.minimum(b, steps - 2), 0, 0)),
            pl.BlockSpec((1, channels, 64), lambda b: (jnp.minimum(b, steps - 2), 0, 0)),
            pl.BlockSpec(weight.shape, fixed3),
            pl.BlockSpec(bias.shape, fixed2),
            pl.BlockSpec(head_bias.shape, fixed2),
            pl.BlockSpec((8, 16, col_count), late),
            pl.BlockSpec(value.shape, fixed3),
            pl.BlockSpec(owner.shape, fixed2),
        ],
        out_specs=[
            pl.BlockSpec((8, channels, col_count), late),
            pl.BlockSpec((row_count, 16, 128), fixed3),
        ],
        out_shape=[
            jax.ShapeDtypeStruct((row_count, channels, col_count), jnp.bfloat16),
            jax.ShapeDtypeStruct((row_count, 16, 128), jnp.float32),
        ],
        scratch_shapes=[
            pltpu.VMEM((4, 8, 3 * channels, col_count), jnp.bfloat16),
            pltpu.VMEM((row_count * 16, col_count), jnp.bfloat16),
            pltpu.VMEM((3, channels, 3 * channels), jnp.bfloat16),
            pltpu.VMEM((16, channels), jnp.bfloat16),
            pltpu.VMEM((channels, col_count), jnp.float32),
        ],
        name="main",
    )(up, own, down, left, right, weight, bias, head_bias, base, value, owner)


def to_global(local, frame):
    span = local.shape[1] // 3
    turned = []
    for x in range(3):
        total = frame[:, 9 + x : 10 + x]
        for d in range(3):
            column = frame[:, 3 * x + d : 3 * x + d + 1]
            total = total + column * local[:, span * d : span * (d + 1)]
        turned.append(total)
    return jnp.concatenate(turned, axis=1)


def keys_kernel(
    single_ref,
    w_key_ref,
    w_value_ref,
    w_kvpts_ref,
    frame_ref,
    pick_key_ref,
    pick_value_ref,
    shift_value_ref,
    points_ref,
    value_ref,
    key_ref,
    key_sq_ref,
):
    rows = single_ref[...]
    key = dot32_nt(rows, w_key_ref[...])
    value = dot32_nt(rows, w_value_ref[...]).astype(jnp.bfloat16)
    frame = frame_columns(frame_ref[...])
    span = w_kvpts_ref.shape[0] // 3
    local = [dot32_nt(rows, w_kvpts_ref[span * d : span * (d + 1), :]) for d in range(3)]
    empty = jnp.zeros((key.shape[0], 384 - key.shape[1]), jnp.float32)
    key_parts = in_pieces(jnp.concatenate([key, empty], axis=1), 3)
    picked = [jnp.zeros((rows.shape[0], 384), jnp.float32) for _ in range(3)]
    values = [dot32(value, shift_value_ref[...]), jnp.zeros((rows.shape[0], 512), jnp.float32)]
    for x in range(3):
        total = frame[:, 9 + x : 10 + x]
        for d in range(3):
            total = total + frame[:, 3 * x + d : 3 * x + d + 1] * local[d]
        parts = in_pieces(total, 3)
        own = slice(span * x, span * (x + 1))
        for index in range(3):
            picked[index] = picked[index] + dot32(parts[index], pick_key_ref[own, :])
        for index in range(2):
            values[index] = values[index] + dot32(parts[index], pick_value_ref[own, :])
    for index in range(3):
        key_ref[index] = (key_parts[index].astype(jnp.float32) + picked[index]).astype(jnp.bfloat16)
    value_ref[0] = values[0].astype(jnp.bfloat16)
    value_ref[1] = values[1].astype(jnp.bfloat16)
    whole = picked[0] + picked[1] + picked[2]
    square = jnp.zeros((16, rows.shape[0]), jnp.float32)
    for part in in_pieces(whole * whole, 3):
        square = square + dot32_nt(points_ref[...], part)
    key_sq_ref[...] = square


def keys(single, w_key, w_value, w_kvpts, frame, pick_key, pick_value, shift_value, points):
    count = single.shape[0]
    return pl.pallas_call(
        keys_kernel,
        out_shape=[
            jax.ShapeDtypeStruct((2, count, 512), jnp.bfloat16),
            jax.ShapeDtypeStruct((3, count, 384), jnp.bfloat16),
            jax.ShapeDtypeStruct((16, count), jnp.float32),
        ],
        name="keys",
    )(single, w_key, w_value, w_kvpts, frame, pick_key, pick_value, shift_value, points)


def base_kernel(
    query_ref,
    w_query_ref,
    w_qpts_ref,
    key_ref,
    key_sq_ref,
    table_ref,
    params_ref,
    key_row_ref,
    base_ref,
    frame_ref,
):
    every = query_ref.shape[0] - 24
    tail = query_ref[every:, 0:every].astype(jnp.float32)
    frames = frame_columns(tail[0:8] + tail[8:16] + tail[16:24])
    frame_ref[...] = frames
    joined_keys = jnp.concatenate([key_ref[b] for b in (0, 1, 2, 0, 1, 0)], axis=1)
    point_scale = as_column(params_ref[2:3, :], 16)
    chain = as_column(params_ref[3:4, :], 16)
    shared = 0.5 * point_scale * key_sq_ref[...] + key_row_ref[7:8, :]
    for chunk in range(every // 16):
        base_chunk(
            slice(16 * chunk, 16 * chunk + 16),
            frames,
            joined_keys,
            point_scale,
            chain,
            shared,
            query_ref,
            w_query_ref,
            w_qpts_ref,
            table_ref,
            key_row_ref,
            base_ref,
        )


def base_chunk(
    own,
    frames,
    joined_keys,
    point_scale,
    chain,
    shared,
    query_ref,
    w_query_ref,
    w_qpts_ref,
    table_ref,
    key_row_ref,
    base_ref,
):
    count = 16
    rows = query_ref[own, :]
    frame = frames[own, :]
    query = dot32_nt(rows, w_query_ref[...])
    points = to_global(dot32_nt(rows, w_qpts_ref[...]), frame)
    empty = jnp.zeros((count, 384 - query.shape[1] - points.shape[1]), jnp.float32)
    lane = lax.broadcasted_iota(jnp.int32, table_ref.shape, 1)
    table = table_ref[...] * jnp.where(lane < query.shape[1], 1.0, point_scale)
    features = jnp.concatenate([query, points, empty], axis=1)
    scaled = features[:, None, :] * table[None]
    placed = jnp.concatenate([jnp.zeros_like(query), points, empty], axis=1)
    own_sq = 0.5 * jnp.sum(scaled * placed[:, None, :], axis=2, keepdims=True)
    joined = in_pieces(scaled.reshape(count * 16, 384), 3)
    total = dot32_nt(
        jnp.concatenate([joined[a] for a in (0, 0, 0, 1, 1, 2)], axis=1), joined_keys
    )
    same = (frame[:, 12:13] == key_row_ref[6:7, :]).astype(jnp.float32)
    base_ref[own] = (
        total.reshape(count, 16, -1) - own_sq - shared[None] + chain[None] * same[:, None, :]
    )


def base_logits(query, w_query, w_qpts, key, key_sq, table, params, key_row):
    count = query.shape[0] - 24
    return pl.pallas_call(
        base_kernel,
        out_shape=[
            jax.ShapeDtypeStruct((count, 16, key.shape[1]), jnp.float32),
            jax.ShapeDtypeStruct((count, 16), jnp.float32),
        ],
        name="base",
    )(query, w_query, w_qpts, key, key_sq, table, params, key_row)


def finish_kernel(
    sums_ref, owner_ref, frame_ref, message_ref, w_out_ref, params_ref, out_ref
):
    sums = sums_ref[...]
    parts, count = sums.shape[0], sums.shape[1]
    width = message_ref.shape[1]
    place = lax.axis_index("col") * count
    marks = sums[:, :, 15, :]
    lane = lax.broadcasted_iota(jnp.int32, (1, 1, 128), 2)
    live = jnp.logical_and(lane >= 96, lane < 108)
    grown = jnp.exp(marks - jnp.max(marks, axis=0, keepdims=True))
    moved = pltpu.roll(grown.reshape(parts * count, 128), 12, 1).reshape(parts, count, 128)
    totals = pltpu.roll(jnp.sum(marks * moved, axis=0), 116, 1)[None]
    scales = jnp.where(live, grown / jnp.where(live, totals, 1.0), 0.0)
    turned = 96 + lax.broadcasted_iota(jnp.int32, (16, 128), 0) == lax.broadcasted_iota(
        jnp.int32, (16, 128), 1
    )
    columns = jnp.sum(
        jnp.where(turned[None, None], scales[:, :, None, :], 0.0), axis=3, keepdims=True
    )
    means = jnp.sum(sums * columns, axis=0)
    rows = scales.reshape(parts * count, 128)
    owner = jnp.concatenate(
        [
            jnp.zeros((96, owner_ref.shape[1]), jnp.float32),
            owner_ref[...],
            jnp.zeros((16, owner_ref.shape[1]), jnp.float32),
        ],
        axis=0,
    ).astype(jnp.bfloat16)
    lanes = jnp.zeros((parts * count, owner_ref.shape[1]), jnp.float32)
    for part in reversed(in_pieces(rows, 3)):
        lanes = lanes + dot32(part, owner)
    lanes = lanes.reshape(parts, count, -1)
    flats = [
        jnp.sum(sums[:, :, 12 + k, :] * lanes[:, :, 128 * k : 128 * k + 128], axis=0)
        for k in range(4)
    ]
    flat = jnp.concatenate(flats, axis=1)
    frame = frame_ref[pl.ds(pl.multiple_of(place, count), count), :]
    centred = [flat[:, 192 + 96 * x : 288 + 96 * x] - frame[:, 9 + x : 10 + x] for x in range(3)]
    local = [
        sum(frame[:, 3 * x + d : 3 * x + d + 1] * centred[x] for x in range(3)) for d in range(3)
    ]
    features = []
    for h in range(12):
        features += [flat[:, 16 * h : 16 * h + 16], means[:, h, 0:64]]
        features += [part[:, 8 * h : 8 * h + 8] for part in local]
    update = jnp.zeros((count, width), jnp.float32)
    for part in reversed(in_pieces(jnp.concatenate(features, axis=1), 3)):
        update = update + dot32(part, w_out_ref[...])
    shape = (count, message_ref.shape[0])
    mine = lax.broadcasted_iota(jnp.int32, shape, 1) == place + lax.broadcasted_iota(
        jnp.int32, shape, 0
    )
    single = dot32(mine.astype(jnp.bfloat16), message_ref[...])
    hidden = single + update
    row_mean = jnp.mean(hidden, axis=1, keepdims=True)
    row_var = jnp.mean((hidden - row_mean) ** 2, axis=1, keepdims=True)
    rows = ((hidden - row_mean) * lax.rsqrt(row_var + norm_eps) * params_ref[0:1, :]).astype(jnp.bfloat16)
    for index in range(parts):
        out_ref[index] = rows


def finish(sums, owner, frame, message, w_out, params):
    parts, count = sums.shape[:2]
    return pl.pallas_call(
        finish_kernel,
        out_shape=jax.ShapeDtypeStruct((parts, count, message.shape[1]), jnp.bfloat16),
        name="finish",
    )(sums, owner, frame, message, w_out, params)


def pack_kernel(single_ref, quat_ref, trans_ref, chain_ref, mask_ref, message_ref, rows_ref):
    count = message_ref.shape[0] - 24
    width = message_ref.shape[1]
    slots = single_ref.shape[0] // count
    slot = lax.axis_index("row") % slots
    rows_ref[0:3, :] = quat_ref[...]
    rows_ref[3:6, :] = trans_ref[...]
    rows_ref[6:7, :] = chain_ref[...].astype(jnp.float32)[None, :]
    rows_ref[7:8, :] = mask_penalty * (1.0 - mask_ref[...].astype(jnp.float32)[None, :])
    message_ref[0:count, :] = single_ref[pl.ds(pl.multiple_of(slot * count, count), count), :]
    rows = rows_ref[:, 0:count]
    for k in range(1, slots):
        rows = jnp.where(slot == k, rows_ref[:, k * count : (k + 1) * count], rows)
    rows = jnp.concatenate([rows, jnp.zeros((rows.shape[0], width - count), jnp.float32)], axis=1)
    for k, part in enumerate(in_pieces(rows, 3)):
        message_ref[count + 8 * k : count + 8 * k + 8, :] = part


def pack(single, quat_vec, trans, chain_id, residue_mask, count):
    return pl.pallas_call(
        pack_kernel,
        out_shape=[
            jax.ShapeDtypeStruct((count + 24, single.shape[1]), single.dtype),
            jax.ShapeDtypeStruct((8, single.shape[0]), jnp.float32),
        ],
        name="pack",
    )(single, quat_vec, trans, chain_id, residue_mask)


def tables(head_count, head_dim, query_points, value_points):
    both = query_points + value_points
    span = 3 * head_count * both
    pick_key = np.zeros((span, 384), np.float32)
    pick_value = np.zeros((span, 512), np.float32)
    shift_value = np.zeros((head_count * head_dim, 512), np.float32)
    points = np.zeros((16, 384), np.float32)
    scalars = np.zeros((16, 384), np.float32)
    owner = np.zeros((16, 512), np.float32)
    for h in range(head_count):
        for d in range(head_dim):
            lane = h * head_dim + d
            scalars[h, lane] = 1.0
            owner[h, lane] = 1.0
            shift_value[lane, lane] = 1.0
        for x in range(3):
            first = (x * head_count + h) * both
            for p in range(query_points):
                lane = head_count * head_dim + (x * head_count + h) * query_points + p
                pick_key[first + p, lane] = 1.0
                points[h, lane] = 1.0
            for p in range(value_points):
                lane = head_count * head_dim + (x * head_count + h) * value_points + p
                pick_value[first + query_points + p, lane] = 1.0
                owner[h, lane] = 1.0
    return pick_key, pick_value, shift_value, points, scalars, owner


def shifted(cells, axis, forward):
    count = lax.axis_size(axis)
    if forward:
        routes = [(i, i + 1) for i in range(count - 1)]
    else:
        routes = [(i + 1, i) for i in range(count - 1)]
    return lax.ppermute(cells, axis, routes)


def query_routes(n_row, n_col):
    group = n_row // n_col
    pairs = []
    for holder_col in range(n_col):
        for holder in range(n_row):
            slot = holder // group
            half = n_col // 2
            col = slot // half * half + (slot + half // 2) % half
            target = holder_col * group + holder % group
            pairs.append((holder * n_col + holder_col, target * n_col + col))
    return pairs


def per_device(
    pair,
    conv_weight,
    conv_bias,
    single,
    quat_vec,
    trans,
    chain_id,
    residue_mask,
    w_query,
    w_key,
    w_value,
    w_qpts,
    w_kvpts,
    w_bias,
    head_weight,
    chain_weight,
    w_out,
    ln_gain,
):
    channels, row_count, col_count = pair.shape
    head_count = w_bias.shape[0]
    head_dim = w_query.shape[1] // head_count
    width = single.shape[1]
    query_points = w_qpts.shape[1] // (3 * head_count)
    value_points = w_kvpts.shape[1] // (3 * head_count) - query_points
    n_row, n_col = lax.axis_size("row"), lax.axis_size("col")
    part_count = row_count // n_col

    raw_up = shifted(pair[:, row_count - DILATION_STEP :], "row", True)
    raw_down = shifted(pair[:, :DILATION_STEP], "row", False)
    routes = query_routes(n_row, n_col)
    message, rows = pack(single, quat_vec, trans, chain_id, residue_mask, row_count)
    message = lax.ppermute(message, ("row", "col"), routes)
    point_scale = logit_scale * jax.nn.softplus(head_weight) * math.sqrt(2.0 / (9.0 * query_points))
    wide = lambda row: jnp.pad(row, (0, width - row.shape[0]))[None, :]
    params = jnp.concatenate(
        [wide(ln_gain), wide(conv_bias), wide(point_scale), wide(chain_weight)]
        + [jnp.zeros((4, width), jnp.float32)],
        axis=0,
    )
    own, own_head, own_tail = turn(pair)
    pick_key, pick_value, shift_value, points, scalars, owner = tables(
        head_count, head_dim, query_points, value_points
    )
    value, key, key_sq = keys(
        single,
        w_key.T,
        w_value.T,
        w_kvpts.T,
        rows,
        jnp.asarray(pick_key, jnp.bfloat16),
        jnp.asarray(pick_value, jnp.bfloat16),
        jnp.asarray(shift_value, jnp.bfloat16),
        jnp.asarray(points, jnp.bfloat16),
    )
    raw_up, raw_down, key_sq = lax.optimization_barrier((raw_up, raw_down, key_sq))
    up, down, to_left, to_right = rim(raw_up, raw_down, own_head, own_tail)
    to_right, to_left, key_rows = lax.optimization_barrier((to_right, to_left, rows))
    left = shifted(to_right, "col", True)
    right = shifted(to_left, "col", False)
    table = scalars * (logit_scale / math.sqrt(head_dim)) + points
    base, frame = base_logits(
        message,
        w_query.T,
        w_qpts.T,
        key,
        key_sq,
        jnp.asarray(table, jnp.float32),
        params,
        key_rows,
    )
    owner = jnp.asarray(owner, jnp.float32)
    updated, sums = main(
        up,
        own,
        down,
        left,
        right,
        conv_weight,
        params,
        w_bias,
        base,
        value,
        owner,
    )
    pair_out = updated.transpose(1, 0, 2)
    sums = sums.reshape(n_col, part_count, 16, 128)
    sums = lax.all_to_all(sums, "col", 0, 0, tiled=False)
    spread_rows = finish(sums, owner, frame, message, w_out, params)
    single_out = lax.all_to_all(spread_rows, "col", 0, 0, tiled=False).reshape(row_count, width)
    return (pair_out, single_out)


def solution(mesh):
    return jax.shard_map(
        per_device,
        mesh=mesh,
        in_specs=(
            P(None, "row", "col"),
            P(),
            P(),
            P("col", None),
            P(None, "col"),
            P(None, "col"),
            P("col"),
            P("col"),
            P(),
            P(),
            P(),
            P(),
            P(),
            P(),
            P(),
            P(),
            P(),
            P(),
        ),
        out_specs=(P(None, "row", "col"), P("row", None)),
        check_vma=False,
    )
```

```python
import math

import jax
import jax.numpy as jnp
import numpy as np
from jax import lax
from jax.experimental import pallas as pl
from jax.experimental.pallas import tpu as pltpu
from jax.sharding import PartitionSpec as P

DILATION_STEP = 8


logit_scale = math.sqrt(1.0 / 3.0)
mask_penalty = 10000.0
norm_eps = 1e-05
highest = lax.Precision.HIGHEST


def in_pieces(value, count):
    parts = []
    for _ in range(count - 1):
        part = value.astype(jnp.bfloat16)
        parts.append(part)
        value = value - part.astype(jnp.float32)
    parts.append(value.astype(jnp.bfloat16))
    return parts


def dot32(a, b):
    return jnp.dot(a, b, preferred_element_type=jnp.float32)


def dot32_nt(a, b):
    return lax.dot_general(a, b, (((1,), (1,)), ((), ())), preferred_element_type=jnp.float32)


def edge_cells(rows):
    head = jnp.concatenate([row[:, :DILATION_STEP] for row in rows], axis=1)
    tail = jnp.concatenate([row[:, row.shape[1] - DILATION_STEP :] for row in rows], axis=1)
    return head, tail


def turn_kernel(pair_ref, rows_ref, head_ref, tail_ref):
    turned = jnp.swapaxes(pair_ref[...], 0, 1)
    rows_ref[...] = turned
    for block in range(turned.shape[0] // 8):
        head, tail = edge_cells([turned[8 * block + i] for i in range(8)])
        head_ref[block] = head
        tail_ref[block] = tail


def turn(pair):
    channels, row_count, col_count = pair.shape
    step = 16
    edge = jax.ShapeDtypeStruct((row_count // 8, channels, 64), pair.dtype)
    return pl.pallas_call(
        turn_kernel,
        grid=(row_count // step,),
        in_specs=[pl.BlockSpec((channels, step, col_count), lambda b: (0, b, 0))],
        out_specs=[
            pl.BlockSpec((step, channels, col_count), lambda b: (b, 0, 0)),
            pl.BlockSpec((step // 8, channels, 64), lambda b: (b, 0, 0)),
            pl.BlockSpec((step // 8, channels, 64), lambda b: (b, 0, 0)),
        ],
        out_shape=[
            jax.ShapeDtypeStruct((row_count, channels, col_count), pair.dtype),
            edge,
            edge,
        ],
        name="turn",
    )(pair)


def rim_kernel(
    raw_up_ref,
    raw_down_ref,
    own_head_ref,
    own_tail_ref,
    up_ref,
    down_ref,
    to_left_ref,
    to_right_ref,
    near_ref,
    sems,
):
    copies = [
        pltpu.make_async_copy(raw, near_ref.at[k], sems.at[k])
        for k, raw in enumerate((raw_up_ref, raw_down_ref))
    ]
    for copy in copies:
        copy.start()
    inner = own_head_ref.shape[0]
    to_left_ref[1 : 1 + inner] = own_head_ref[...]
    to_right_ref[1 : 1 + inner] = own_tail_ref[...]
    for k, (ref, index) in enumerate(((up_ref, 0), (down_ref, inner + 1))):
        copies[k].wait()
        turned = jnp.swapaxes(near_ref[k], 0, 1)
        ref[...] = turned
        head, tail = edge_cells([turned[i] for i in range(8)])
        to_left_ref[index] = head
        to_right_ref[index] = tail


def rim(raw_up, raw_down, own_head, own_tail):
    channels, count, cols = raw_up.shape
    inner = own_head.shape[0]
    rows = jax.ShapeDtypeStruct((count, channels, cols), raw_up.dtype)
    edge = jax.ShapeDtypeStruct((inner + 2, channels, 64), raw_up.dtype)
    vmem = pl.BlockSpec(memory_space=pltpu.VMEM)
    return pl.pallas_call(
        rim_kernel,
        in_specs=[pl.BlockSpec(memory_space=pl.ANY)] * 2 + [vmem] * 2,
        out_specs=[vmem] * 4,
        out_shape=[rows, rows, edge, edge],
        scratch_shapes=[
            pltpu.VMEM((2, channels, count, cols), raw_up.dtype),
            pltpu.SemaphoreType.DMA((2,)),
        ],
        name="rim",
    )(raw_up, raw_down, own_head, own_tail)


def as_column(row, count):
    shape = (count, row.shape[1])
    same = lax.broadcasted_iota(jnp.int32, shape, 0) == lax.broadcasted_iota(jnp.int32, shape, 1)
    return jnp.sum(jnp.where(same, row, 0.0), axis=1, keepdims=True)


def frame_columns(rows):
    comp_b, comp_c, comp_d = rows[0:1], rows[1:2], rows[2:3]
    bb, cc, dd = comp_b * comp_b, comp_c * comp_c, comp_d * comp_d
    inverse = 1.0 / (1.0 + bb + cc + dd)
    turned = [
        1.0 + bb - cc - dd,
        2.0 * (comp_b * comp_c - comp_d),
        2.0 * (comp_b * comp_d + comp_c),
        2.0 * (comp_b * comp_c + comp_d),
        1.0 - bb + cc - dd,
        2.0 * (comp_c * comp_d - comp_b),
        2.0 * (comp_b * comp_d - comp_c),
        2.0 * (comp_c * comp_d + comp_b),
        1.0 - bb - cc + dd,
    ]
    count = rows.shape[1]
    stacked = jnp.concatenate(
        [part * inverse for part in turned]
        + [rows[3:7], jnp.zeros((3, count), jnp.float32)],
        axis=0,
    )
    shape = (count, count)
    same = lax.broadcasted_iota(jnp.int32, shape, 0) == lax.broadcasted_iota(jnp.int32, shape, 1)
    eye = same.astype(jnp.bfloat16)
    columns = jnp.zeros((count, 16), jnp.float32)
    for part in in_pieces(stacked, 3):
        columns = columns + dot32_nt(eye, part)
    return columns


def main_kernel(
    up_ref,
    own_ref,
    down_ref,
    left_ref,
    right_ref,
    taps_ref,
    params_ref,
    raw_bias_ref,
    base_ref,
    value_ref,
    owner_ref,
    out_ref,
    sums_ref,
    window_ref,
    soft_ref,
    weight_ref,
    head_bias_ref,
    shift_ref,
):
    step = pl.program_id(0)
    last = pl.num_programs(0) - 1
    channels = own_ref.shape[1]
    cols = own_ref.shape[2]
    slot = lax.rem(step, 4)

    def stage(picked=range(8)):
        lane = lax.broadcasted_iota(jnp.int32, (channels, 128), 1)
        empty = jnp.zeros((channels, 64), jnp.bfloat16)
        before = jnp.concatenate([left_ref[0], empty], axis=1)
        after = jnp.concatenate([right_ref[0], empty], axis=1)
        top = channels
        for i in picked:
            cells = jnp.where(
                step == 0, up_ref[i], jnp.where(step == last - 1, down_ref[i], own_ref[i])
            )
            ahead = [pltpu.roll(cells[:, 128 * k : 128 * k + 128], 8, 1) for k in range(2)]
            fill = pltpu.roll(before, (128 - 8 * i) % 128, 1)
            window_ref[slot, i, 0:top, 0:128] = jnp.where(lane < 8, fill, ahead[0])
            window_ref[slot, i, 0:top, 128:256] = jnp.where(lane < 8, ahead[0], ahead[1])
            window_ref[slot, i, top : 2 * top] = cells
            back = [pltpu.roll(cells[:, 128 * k : 128 * k + 128], 120, 1) for k in range(2)]
            fill = pltpu.roll(after, 120 - 8 * i, 1)
            window_ref[slot, i, 2 * top : 3 * top, 0:128] = jnp.where(lane >= 120, back[1], back[0])
            window_ref[slot, i, 2 * top : 3 * top, 128:256] = jnp.where(lane >= 120, fill, back[1])

    @pl.when(step == 0)
    def _():
        for dy in range(3):
            weight_ref[dy] = jnp.concatenate([taps_ref[3 * dy + dx] for dx in range(3)], axis=1)
        heads = raw_bias_ref.shape[0]
        pick = lax.broadcasted_iota(jnp.int32, (16, heads), 0) == lax.broadcasted_iota(
            jnp.int32, (16, heads), 1
        )
        head_bias_ref[...] = dot32(pick.astype(jnp.bfloat16), raw_bias_ref[...]).astype(jnp.bfloat16)
        shift_ref[...] = jnp.broadcast_to(as_column(params_ref[1:2, :], channels), (channels, cols))

    @pl.when(step < 3)
    def _():
        stage()

    @pl.when(step >= 3)
    def _():
        first = lax.rem(step + 1, 4)
        middle = lax.rem(step + 2, 4)
        third = lax.rem(step + 3, 4)
        lane = lax.broadcasted_iota(jnp.int32, (8, 16, 128), 2)

        def convolve(i):
            return (
                jnp.dot(weight_ref[0], window_ref[first, i], preferred_element_type=jnp.float32)
                + jnp.dot(weight_ref[1], window_ref[middle, i], preferred_element_type=jnp.float32)
                + jnp.dot(weight_ref[2], window_ref[third, i], preferred_element_type=jnp.float32)
            )

        shift = shift_ref[...]
        pending = convolve(0)
        for i in range(8):
            conv = pending + shift
            if i < 7:
                pending = convolve(i + 1)
            bent = jnp.where(conv > 0.0, conv, jnp.exp(jnp.minimum(conv, 0.0)) - 1.0)
            cells = window_ref[middle, i, channels : 2 * channels].astype(jnp.float32)
            out_ref[i] = (cells + bent).astype(jnp.bfloat16)
            stage((i,))
        bias = jnp.stack(
            [
                jnp.dot(head_bias_ref[...], out_ref[i], preferred_element_type=jnp.float32)
                for i in range(8)
            ]
        )
        logits = base_ref[...] + logit_scale * bias
        peak = jnp.max(logits, axis=2, keepdims=True)
        weights = jnp.exp(logits - peak).astype(jnp.bfloat16)
        total = jnp.sum(weights.astype(jnp.float32), axis=2, keepdims=True)
        pair_sum = jnp.stack(
            [
                lax.dot_general(
                    weights[i],
                    out_ref[i],
                    (((1,), (1,)), ((), ())),
                    preferred_element_type=jnp.float32,
                )
                for i in range(8)
            ]
        )
        padded = jnp.concatenate([pair_sum, jnp.zeros((8, 16, 64), jnp.float32)], axis=2)
        row = pl.multiple_of((step - 3) * 8, 8)
        sums_ref[pl.ds(row, 8)] = jnp.where(
            lane == 104, peak, jnp.where(lane == 105, total, padded)
        )
        soft_ref[pl.ds(pl.multiple_of(row * 16, 128), 128), :] = weights.reshape(128, cols)

    @pl.when(step == last)
    def _():
        chunk = 256
        sub = lax.broadcasted_iota(jnp.int32, (chunk // 16, 16, 128), 1)
        lane = lax.broadcasted_iota(jnp.int32, (chunk // 16, 16, 128), 2)
        for part in range(soft_ref.shape[0] // chunk):
            soft = soft_ref[part * chunk : (part + 1) * chunk, :]
            acc = jnp.dot(soft, value_ref[0], preferred_element_type=jnp.float32) + jnp.dot(
                soft, value_ref[1], preferred_element_type=jnp.float32
            )
            acc = acc.reshape(chunk // 16, 16, 512) * owner_ref[...][None]
            folded = jnp.sum(acc, axis=1, keepdims=True)
            rows = slice(part * chunk // 16, (part + 1) * chunk // 16)
            kept = sums_ref[rows]
            marks = jnp.where(
                lane == 96 + sub,
                kept[:, :, 104:105],
                jnp.where(lane == 108 + sub, kept[:, :, 105:106], 0.0),
            )
            marks = jnp.sum(jnp.where(sub < 12, marks, 0.0), axis=1, keepdims=True)
            for k in range(4):
                lanes = folded[:, :, 128 * k : 128 * k + 128]
                if k == 3:
                    lanes = lanes + marks
                kept = jnp.where(sub == 12 + k, lanes, kept)
            sums_ref[rows] = kept


def main(up, own, down, left, right, weight, bias, head_bias, base, value, owner):
    row_count, channels, col_count = own.shape
    steps = row_count // 8 + 3
    fixed3 = lambda b: (0, 0, 0)
    fixed2 = lambda b: (0, 0)
    late = lambda b: (jnp.maximum(b - 3, 0), 0, 0)
    return pl.pallas_call(
        main_kernel,
        grid=(steps,),
        in_specs=[
            pl.BlockSpec(up.shape, fixed3),
            pl.BlockSpec((8, channels, col_count), lambda b: (jnp.clip(b - 1, 0, steps - 4), 0, 0)),
            pl.BlockSpec(down.shape, fixed3),
            pl.BlockSpec((1, channels, 64), lambda b: (jnp.minimum(b, steps - 2), 0, 0)),
            pl.BlockSpec((1, channels, 64), lambda b: (jnp.minimum(b, steps - 2), 0, 0)),
            pl.BlockSpec(weight.shape, fixed3),
            pl.BlockSpec(bias.shape, fixed2),
            pl.BlockSpec(head_bias.shape, fixed2),
            pl.BlockSpec((8, 16, col_count), late),
            pl.BlockSpec(value.shape, fixed3),
            pl.BlockSpec(owner.shape, fixed2),
        ],
        out_specs=[
            pl.BlockSpec((8, channels, col_count), late),
            pl.BlockSpec((row_count, 16, 128), fixed3),
        ],
        out_shape=[
            jax.ShapeDtypeStruct((row_count, channels, col_count), jnp.bfloat16),
            jax.ShapeDtypeStruct((row_count, 16, 128), jnp.float32),
        ],
        scratch_shapes=[
            pltpu.VMEM((4, 8, 3 * channels, col_count), jnp.bfloat16),
            pltpu.VMEM((row_count * 16, col_count), jnp.bfloat16),
            pltpu.VMEM((3, channels, 3 * channels), jnp.bfloat16),
            pltpu.VMEM((16, channels), jnp.bfloat16),
            pltpu.VMEM((channels, col_count), jnp.float32),
        ],
        name="main",
    )(up, own, down, left, right, weight, bias, head_bias, base, value, owner)


def to_global(local, frame):
    span = local.shape[1] // 3
    turned = []
    for x in range(3):
        total = frame[:, 9 + x : 10 + x]
        for d in range(3):
            column = frame[:, 3 * x + d : 3 * x + d + 1]
            total = total + column * local[:, span * d : span * (d + 1)]
        turned.append(total)
    return jnp.concatenate(turned, axis=1)


def keys_kernel(
    single_ref,
    w_key_ref,
    w_value_ref,
    w_kvpts_ref,
    frame_ref,
    pick_key_ref,
    pick_value_ref,
    points_ref,
    value_ref,
    key_ref,
    key_sq_ref,
):
    rows = single_ref[...]
    key = dot32_nt(rows, w_key_ref[...])
    value = dot32_nt(rows, w_value_ref[...]).astype(jnp.bfloat16)
    frame = frame_columns(frame_ref[...])
    span = w_kvpts_ref.shape[0] // 3
    local = [dot32_nt(rows, w_kvpts_ref[span * d : span * (d + 1), :]) for d in range(3)]
    empty = jnp.zeros((key.shape[0], 384 - key.shape[1]), jnp.float32)
    key_parts = in_pieces(jnp.concatenate([key, empty], axis=1), 3)
    empty = jnp.zeros((key.shape[0], 512 - value.shape[1]), jnp.float32)
    whole_value = jnp.concatenate([value.astype(jnp.float32), empty], axis=1)
    picked = [jnp.zeros((rows.shape[0], 256), jnp.float32) for _ in range(3)]
    values = [whole_value, jnp.zeros((rows.shape[0], 512), jnp.float32)]
    for x in range(3):
        total = frame[:, 9 + x : 10 + x]
        for d in range(3):
            total = total + frame[:, 3 * x + d : 3 * x + d + 1] * local[d]
        parts = in_pieces(total, 3)
        own = slice(span * x, span * (x + 1))
        for index in range(3):
            picked[index] = picked[index] + dot32(parts[index], pick_key_ref[own, :])
        for index in range(2):
            values[index] = values[index] + dot32(parts[index], pick_value_ref[own, :])
    for index in range(3):
        part = key_parts[index]
        key_ref[index, :, 0:128] = part[:, 0:128]
        key_ref[index, :, 128:384] = (part[:, 128:384].astype(jnp.float32) + picked[index]).astype(
            jnp.bfloat16
        )
    value_ref[0] = values[0].astype(jnp.bfloat16)
    value_ref[1] = values[1].astype(jnp.bfloat16)
    whole = picked[0] + picked[1] + picked[2]
    square = jnp.zeros((16, rows.shape[0]), jnp.float32)
    for part in in_pieces(whole * whole, 3):
        square = square + dot32_nt(points_ref[...], part)
    key_sq_ref[...] = square


def keys(single, w_key, w_value, w_kvpts, frame, pick_key, pick_value, points):
    count = single.shape[0]
    return pl.pallas_call(
        keys_kernel,
        out_shape=[
            jax.ShapeDtypeStruct((2, count, 512), jnp.bfloat16),
            jax.ShapeDtypeStruct((3, count, 384), jnp.bfloat16),
            jax.ShapeDtypeStruct((16, count), jnp.float32),
        ],
        name="keys",
    )(single, w_key, w_value, w_kvpts, frame, pick_key, pick_value, points)


def base_kernel(
    query_ref,
    w_query_ref,
    w_qpts_ref,
    key_ref,
    key_sq_ref,
    table_ref,
    params_ref,
    key_row_ref,
    base_ref,
    frame_ref,
):
    every = query_ref.shape[0] - 24
    tail = query_ref[every:, 0:every].astype(jnp.float32)
    frames = frame_columns(tail[0:8] + tail[8:16] + tail[16:24])
    frame_ref[...] = frames
    joined_keys = jnp.concatenate([key_ref[b] for b in (0, 1, 2, 0, 1, 0)], axis=1)
    point_scale = as_column(params_ref[2:3, :], 16)
    chain = as_column(params_ref[3:4, :], 16)
    shared = 0.5 * point_scale * key_sq_ref[...] + key_row_ref[7:8, :]
    for chunk in range(every // 16):
        base_chunk(
            slice(16 * chunk, 16 * chunk + 16),
            frames,
            joined_keys,
            point_scale,
            chain,
            shared,
            query_ref,
            w_query_ref,
            w_qpts_ref,
            table_ref,
            key_row_ref,
            base_ref,
        )


def base_chunk(
    own,
    frames,
    joined_keys,
    point_scale,
    chain,
    shared,
    query_ref,
    w_query_ref,
    w_qpts_ref,
    table_ref,
    key_row_ref,
    base_ref,
):
    count = 16
    rows = query_ref[own, :]
    frame = frames[own, :]
    query = dot32_nt(rows, w_query_ref[...])
    points = to_global(dot32_nt(rows, w_qpts_ref[...]), frame)
    empty = jnp.zeros((count, 384 - query.shape[1] - points.shape[1]), jnp.float32)
    lane = lax.broadcasted_iota(jnp.int32, table_ref.shape, 1)
    table = table_ref[...] * jnp.where(lane < query.shape[1], 1.0, point_scale)
    features = jnp.concatenate([query, points, empty], axis=1)
    scaled = features[:, None, :] * table[None]
    placed = jnp.concatenate([jnp.zeros_like(query), points, empty], axis=1)
    own_sq = 0.5 * jnp.sum(scaled * placed[:, None, :], axis=2, keepdims=True)
    joined = in_pieces(scaled.reshape(count * 16, 384), 3)
    total = dot32_nt(
        jnp.concatenate([joined[a] for a in (0, 0, 0, 1, 1, 2)], axis=1), joined_keys
    )
    same = (frame[:, 12:13] == key_row_ref[6:7, :]).astype(jnp.float32)
    base_ref[own] = (
        total.reshape(count, 16, -1) - own_sq - shared[None] + chain[None] * same[:, None, :]
    )


def base_logits(query, w_query, w_qpts, key, key_sq, table, params, key_row):
    count = query.shape[0] - 24
    return pl.pallas_call(
        base_kernel,
        out_shape=[
            jax.ShapeDtypeStruct((count, 16, key.shape[1]), jnp.float32),
            jax.ShapeDtypeStruct((count, 16), jnp.float32),
        ],
        name="base",
    )(query, w_query, w_qpts, key, key_sq, table, params, key_row)


def finish_kernel(
    sums_ref, owner_ref, frame_ref, message_ref, w_out_ref, params_ref, out_ref
):
    sums = sums_ref[...]
    parts, count = sums.shape[0], sums.shape[1]
    width = message_ref.shape[1]
    place = lax.axis_index("col") * count
    marks = sums[:, :, 15, :]
    lane = lax.broadcasted_iota(jnp.int32, (1, 1, 128), 2)
    live = jnp.logical_and(lane >= 96, lane < 108)
    grown = jnp.exp(marks - jnp.max(marks, axis=0, keepdims=True))
    moved = pltpu.roll(grown.reshape(parts * count, 128), 12, 1).reshape(parts, count, 128)
    totals = pltpu.roll(jnp.sum(marks * moved, axis=0), 116, 1)[None]
    scales = jnp.where(live, grown / jnp.where(live, totals, 1.0), 0.0)
    turned = 96 + lax.broadcasted_iota(jnp.int32, (16, 128), 0) == lax.broadcasted_iota(
        jnp.int32, (16, 128), 1
    )
    columns = jnp.sum(
        jnp.where(turned[None, None], scales[:, :, None, :], 0.0), axis=3, keepdims=True
    )
    means = jnp.sum(sums * columns, axis=0)
    rows = scales.reshape(parts * count, 128)
    owner = jnp.concatenate(
        [
            jnp.zeros((96, owner_ref.shape[1]), jnp.float32),
            owner_ref[...],
            jnp.zeros((16, owner_ref.shape[1]), jnp.float32),
        ],
        axis=0,
    ).astype(jnp.bfloat16)
    lanes = jnp.zeros((parts * count, owner_ref.shape[1]), jnp.float32)
    for part in reversed(in_pieces(rows, 3)):
        lanes = lanes + dot32(part, owner)
    lanes = lanes.reshape(parts, count, -1)
    flats = [
        jnp.sum(sums[:, :, 12 + k, :] * lanes[:, :, 128 * k : 128 * k + 128], axis=0)
        for k in range(4)
    ]
    flat = jnp.concatenate(flats, axis=1)
    frame = frame_ref[pl.ds(pl.multiple_of(place, count), count), :]
    centred = [flat[:, 192 + 96 * x : 288 + 96 * x] - frame[:, 9 + x : 10 + x] for x in range(3)]
    local = [
        sum(frame[:, 3 * x + d : 3 * x + d + 1] * centred[x] for x in range(3)) for d in range(3)
    ]
    features = []
    for h in range(12):
        features += [flat[:, 16 * h : 16 * h + 16], means[:, h, 0:64]]
        features += [part[:, 8 * h : 8 * h + 8] for part in local]
    update = jnp.zeros((count, width), jnp.float32)
    for part in reversed(in_pieces(jnp.concatenate(features, axis=1), 3)):
        update = update + dot32(part, w_out_ref[...])
    shape = (count, message_ref.shape[0])
    mine = lax.broadcasted_iota(jnp.int32, shape, 1) == place + lax.broadcasted_iota(
        jnp.int32, shape, 0
    )
    single = dot32(mine.astype(jnp.bfloat16), message_ref[...])
    hidden = single + update
    row_mean = jnp.mean(hidden, axis=1, keepdims=True)
    row_var = jnp.mean((hidden - row_mean) ** 2, axis=1, keepdims=True)
    rows = ((hidden - row_mean) * lax.rsqrt(row_var + norm_eps) * params_ref[0:1, :]).astype(jnp.bfloat16)
    for index in range(parts):
        out_ref[index] = rows


def finish(sums, owner, frame, message, w_out, params):
    parts, count = sums.shape[:2]
    return pl.pallas_call(
        finish_kernel,
        out_shape=jax.ShapeDtypeStruct((parts, count, message.shape[1]), jnp.bfloat16),
        name="finish",
    )(sums, owner, frame, message, w_out, params)


def pack_kernel(single_ref, quat_ref, trans_ref, chain_ref, mask_ref, message_ref, rows_ref):
    count = message_ref.shape[0] - 24
    width = message_ref.shape[1]
    slots = single_ref.shape[0] // count
    slot = lax.axis_index("row") % slots
    rows_ref[0:3, :] = quat_ref[...]
    rows_ref[3:6, :] = trans_ref[...]
    rows_ref[6:7, :] = chain_ref[...].astype(jnp.float32)[None, :]
    rows_ref[7:8, :] = mask_penalty * (1.0 - mask_ref[...].astype(jnp.float32)[None, :])
    message_ref[0:count, :] = single_ref[pl.ds(pl.multiple_of(slot * count, count), count), :]
    rows = rows_ref[:, 0:count]
    for k in range(1, slots):
        rows = jnp.where(slot == k, rows_ref[:, k * count : (k + 1) * count], rows)
    rows = jnp.concatenate([rows, jnp.zeros((rows.shape[0], width - count), jnp.float32)], axis=1)
    for k, part in enumerate(in_pieces(rows, 3)):
        message_ref[count + 8 * k : count + 8 * k + 8, :] = part


def pack(single, quat_vec, trans, chain_id, residue_mask, count):
    return pl.pallas_call(
        pack_kernel,
        out_shape=[
            jax.ShapeDtypeStruct((count + 24, single.shape[1]), single.dtype),
            jax.ShapeDtypeStruct((8, single.shape[0]), jnp.float32),
        ],
        name="pack",
    )(single, quat_vec, trans, chain_id, residue_mask)


def tables(head_count, head_dim, query_points, value_points):
    both = query_points + value_points
    span = 3 * head_count * both
    pick_key = np.zeros((span, 384), np.float32)
    pick_value = np.zeros((span, 512), np.float32)
    points = np.zeros((16, 384), np.float32)
    scalars = np.zeros((16, 384), np.float32)
    owner = np.zeros((16, 512), np.float32)
    for h in range(head_count):
        for d in range(head_dim):
            lane = h * head_dim + d
            scalars[h, lane] = 1.0
            owner[h, lane] = 1.0
        for x in range(3):
            first = (x * head_count + h) * both
            for p in range(query_points):
                lane = head_count * head_dim + (x * head_count + h) * query_points + p
                pick_key[first + p, lane] = 1.0
                points[h, lane] = 1.0
            for p in range(value_points):
                lane = head_count * head_dim + (x * head_count + h) * value_points + p
                pick_value[first + query_points + p, lane] = 1.0
                owner[h, lane] = 1.0
    return pick_key, pick_value, points, scalars, owner


def shifted(cells, axis, forward):
    count = lax.axis_size(axis)
    if forward:
        routes = [(i, i + 1) for i in range(count - 1)]
    else:
        routes = [(i + 1, i) for i in range(count - 1)]
    return lax.ppermute(cells, axis, routes)


def query_routes(n_row, n_col):
    group = n_row // n_col
    pairs = []
    for holder_col in range(n_col):
        for holder in range(n_row):
            slot = holder // group
            half = n_col // 2
            col = slot // half * half + (slot + half // 2) % half
            target = holder_col * group + holder % group
            pairs.append((holder * n_col + holder_col, target * n_col + col))
    return pairs


def per_device(
    pair,
    conv_weight,
    conv_bias,
    single,
    quat_vec,
    trans,
    chain_id,
    residue_mask,
    w_query,
    w_key,
    w_value,
    w_qpts,
    w_kvpts,
    w_bias,
    head_weight,
    chain_weight,
    w_out,
    ln_gain,
):
    channels, row_count, col_count = pair.shape
    head_count = w_bias.shape[0]
    head_dim = w_query.shape[1] // head_count
    width = single.shape[1]
    query_points = w_qpts.shape[1] // (3 * head_count)
    value_points = w_kvpts.shape[1] // (3 * head_count) - query_points
    n_row, n_col = lax.axis_size("row"), lax.axis_size("col")
    part_count = row_count // n_col

    raw_up = shifted(pair[:, row_count - DILATION_STEP :], "row", True)
    raw_down = shifted(pair[:, :DILATION_STEP], "row", False)
    routes = query_routes(n_row, n_col)
    message, rows = pack(single, quat_vec, trans, chain_id, residue_mask, row_count)
    message = lax.ppermute(message, ("row", "col"), routes)
    point_scale = logit_scale * jax.nn.softplus(head_weight) * math.sqrt(2.0 / (9.0 * query_points))
    wide = lambda row: jnp.pad(row, (0, width - row.shape[0]))[None, :]
    params = jnp.concatenate(
        [wide(ln_gain), wide(conv_bias), wide(point_scale), wide(chain_weight)]
        + [jnp.zeros((4, width), jnp.float32)],
        axis=0,
    )
    own, own_head, own_tail = turn(pair)
    pick_key, pick_value, points, scalars, owner = tables(
        head_count, head_dim, query_points, value_points
    )
    value, key, key_sq = keys(
        single,
        w_key.T,
        w_value.T,
        w_kvpts.T,
        rows,
        jnp.asarray(pick_key[:, 128:], jnp.bfloat16),
        jnp.asarray(pick_value, jnp.bfloat16),
        jnp.asarray(points[:, 128:], jnp.bfloat16),
    )
    raw_up, raw_down, key_sq = lax.optimization_barrier((raw_up, raw_down, key_sq))
    up, down, to_left, to_right = rim(raw_up, raw_down, own_head, own_tail)
    to_right, to_left, key_rows = lax.optimization_barrier((to_right, to_left, rows))
    left = shifted(to_right, "col", True)
    right = shifted(to_left, "col", False)
    table = scalars * (logit_scale / math.sqrt(head_dim)) + points
    base, frame = base_logits(
        message,
        w_query.T,
        w_qpts.T,
        key,
        key_sq,
        jnp.asarray(table, jnp.float32),
        params,
        key_rows,
    )
    owner = jnp.asarray(owner, jnp.float32)
    updated, sums = main(
        up,
        own,
        down,
        left,
        right,
        conv_weight,
        params,
        w_bias,
        base,
        value,
        owner,
    )
    pair_out = updated.transpose(1, 0, 2)
    sums = sums.reshape(n_col, part_count, 16, 128)
    sums = lax.all_to_all(sums, "col", 0, 0, tiled=False)
    spread_rows = finish(sums, owner, frame, message, w_out, params)
    single_out = lax.all_to_all(spread_rows, "col", 0, 0, tiled=False).reshape(row_count, width)
    return (pair_out, single_out)


def solution(mesh):
    return jax.shard_map(
        per_device,
        mesh=mesh,
        in_specs=(
            P(None, "row", "col"),
            P(),
            P(),
            P("col", None),
            P(None, "col"),
            P(None, "col"),
            P("col"),
            P("col"),
            P(),
            P(),
            P(),
            P(),
            P(),
            P(),
            P(),
            P(),
            P(),
            P(),
        ),
        out_specs=(P(None, "row", "col"), P("row", None)),
        check_vma=False,
    )
```
